512 devices in a mesh: tm: 128 (over y, z, core), rows: 4 (over x).
Axes of the slice: x: 4, y: 8, z: 8, core: 2. Of those that a mesh axis runs over, the one named last changes fastest.
Arguments:
- source_term: float32 [128, 128, 1024], P('tm', 'rows'), may hold values from -6 to 6
- iterate: float32 [128, 128, 1024], P('tm', 'rows'), may hold values from -6 to 6
- initial: float32 [128, 1024], P('rows'), may hold values from -6 to 6
- conductivity: float32 [128, 1024], P('rows'), may hold values from 0.25 to 2
Outputs:
- correction: float32 [128, 128, 1024], P('tm', 'rows')
The draws below stay inside these ranges and needn't reach their ends.
All inputs are finite; a program needn't handle non-finite values.
Results may differ from the reference program's by a relative error of at most 0.0003.
Values sent between devices are 32-bit elements; how exact they have to be, the bound alone decides.
A program may use at most 64 MiB of HBM per device.

```python
import math
import jax
import jax.numpy as jnp
from jax import lax

NC = 1024
SWEEPS = 6
STEPS = 128
NR = 128


def draw_source_term(key, part):
    return jax.random.truncated_normal(key, -6.0, 6.0, (STEPS, NR, NC), jnp.float32)


def draw_conductivity(key, part):
    exponent = jax.random.uniform(key, (NR, NC), jnp.float32, math.log(0.25), math.log(2.0))
    return jnp.clip(jnp.exp(exponent), 0.25, 2.0)


def steps_of(rng, extent, split, low, top_value):
    level = 1.0
    for position, blocks in split:
        heights = jax.random.uniform(jax.random.fold_in(jax.random.fold_in(rng, 6), position), (blocks,), jnp.float32, low / len(split), top_value / len(split))
        level = level * jnp.repeat(jnp.exp(heights), extent[position] // blocks).reshape((-1,) + (1,) * (len(extent) - 1 - position))
    return level


def centred(stream_key, dims, spread, limit, cuts=(), kind=jnp.bfloat16):
    factor_of = steps_of(stream_key, dims, cuts, -0.22, 0.18) if cuts else 1.0
    values = jax.random.normal(stream_key, dims, jnp.float32) * spread * factor_of
    return jnp.minimum(jnp.maximum(values, -limit), limit).astype(kind)


def setup_inputs(seed: int = 0) -> dict:
    arg_keys = jax.random.split(jax.random.key(seed), 5)
    return {
        "source_term": draw_source_term(jax.random.fold_in(arg_keys[4], 71), 0),
        "iterate": centred(arg_keys[1], (STEPS, NR, NC), 1.0, 6.0, ((0, 128), (1, 4)), jnp.float32),
        "initial": centred(arg_keys[2], (NR, NC), 1.0, 6.0, ((0, 4),), jnp.float32),
        "conductivity": draw_conductivity(jax.random.fold_in(arg_keys[4], 71), 0),
    }


time_step = 0.5
wrap_factor = 0.25
chebyshev_spread = 0.7


def sweep_weights(count):
    return [1.0 / (1.0 + chebyshev_spread * math.cos(math.pi * (2 * sweep + 1) / (2 * count))) for sweep in range(count)]


def build_tables(window):
    freq_index = jnp.arange(window, dtype=jnp.int32)
    products = (freq_index[:, None] * freq_index[None, :]) % window
    angles = products.astype(jnp.float32) * (2.0 * math.pi / window)
    cosine = jnp.cos(angles)
    sine = jnp.sin(angles)
    middle = window // 2
    keep_real = (freq_index <= middle).astype(jnp.float32)
    keep_imag = ((freq_index >= 1) & (freq_index < middle)).astype(jnp.float32)
    weighting = jnp.exp(freq_index.astype(jnp.float32) * (math.log(wrap_factor) / window))
    forward = jnp.stack([cosine * keep_real[:, None] * weighting[None, :], -sine * keep_imag[:, None] * weighting[None, :]])
    multiplicity = keep_real * (1.0 + keep_imag)
    scale_back = 1.0 / (window * weighting)
    inverse = jnp.stack([cosine.T * multiplicity[None, :], -sine.T * (2.0 * keep_imag)[None, :]], axis=1) * scale_back[:, None, None]
    root_factor = math.exp(math.log(wrap_factor) / window)
    base_angles = freq_index.astype(jnp.float32) * (2.0 * math.pi / window)
    shift_real = 1.0 - root_factor * jnp.cos(base_angles)
    shift_coupling = root_factor * jnp.sin(base_angles) * keep_imag
    return forward, inverse, shift_real, shift_coupling


def laplace(field):
    widths = [(0, 0)] * (field.ndim - 2) + [(1, 1), (1, 1)]
    padded = jnp.pad(field, widths)
    return 4.0 * field - padded[..., :-2, 1:-1] - padded[..., 2:, 1:-1] - padded[..., 1:-1, :-2] - padded[..., 1:-1, 2:]


def relax(source_pair, shift_one, shift_two, coupling, conductivity):
    diffusion = time_step * conductivity
    diag_one = shift_one + 4.0 * diffusion
    diag_two = shift_two + 4.0 * diffusion
    determinant = diag_one * diag_two + coupling * coupling
    field_real = jnp.zeros_like(source_pair[0])
    field_imag = jnp.zeros_like(source_pair[1])
    for sweep, weight in enumerate(sweep_weights(SWEEPS)):
        if sweep == 0:
            defect_real = source_pair[0]
            defect_imag = source_pair[1]
        else:
            defect_real = source_pair[0] - (shift_one * field_real + diffusion * laplace(field_real) - coupling * field_imag)
            defect_imag = source_pair[1] - (shift_two * field_imag + diffusion * laplace(field_imag) + coupling * field_real)
        field_real = field_real + weight * (diag_two * defect_real + coupling * defect_imag) / determinant
        field_imag = field_imag + weight * (diag_one * defect_imag - coupling * defect_real) / determinant
    return jnp.stack([field_real, field_imag])


def reference(source_term, iterate, initial, conductivity):
    window = STEPS
    forward, inverse, shift_real, shift_coupling = build_tables(window)
    count = window // 2 + 1
    previous = jnp.concatenate([initial[None], iterate[:-1]], axis=0)
    residual = source_term - (iterate + time_step * conductivity * laplace(iterate) - previous)
    spectrum = jnp.einsum("ckn,nrw->kcrw", forward[:, :count], residual, precision=lax.Precision.HIGHEST)

    def solve_one(packed):
        pair, shift_one, coupling = packed
        return relax(pair, shift_one, shift_one, coupling, conductivity)

    solved = lax.map(solve_one, (spectrum, shift_real[:count], shift_coupling[:count]))
    return jnp.einsum("nck,kcrw->nrw", inverse[:, :, :count], solved, precision=lax.Precision.HIGHEST)
```

```python
import functools
import math

import jax
import jax.numpy as jnp
import numpy as np
from jax import lax
from jax.experimental import pallas as pl
from jax.experimental.pallas import tpu as pltpu
from jax.sharding import PartitionSpec as P

MESH = pl.DeviceIdType.MESH

SWEEPS = 6
time_step = 0.5
wrap_factor = 0.25
chebyshev_spread = 0.7

STEPS = 128
COLS = 1024
ROWS = 32
TILE = 8
HALO = SWEEPS - 1
SPAN = TILE + 2 * HALO
GROUPS = 7
DEPTH = 6
TOP = 8 - HALO
FRAME = ROWS + 16


def sweep_weights(count):
    return [
        1.0 / (1.0 + chebyshev_spread * math.cos(math.pi * (2 * sweep + 1) / (2 * count)))
        for sweep in range(count)
    ]


def tables():
    half = STEPS // 2
    k = np.arange(half)
    n = np.arange(STEPS)
    angle = 2.0 * np.pi * (k[:, None] * n[None, :] % STEPS) / STEPS
    weight = wrap_factor ** (n / STEPS)
    cosine, sine = np.cos(angle), np.sin(angle)
    alternating = np.where(n % 2 == 0, 1.0, -1.0)
    forward = np.concatenate([cosine, -sine]) * weight
    forward[half] = alternating * weight
    multiplicity = np.where(k == 0, 1.0, 2.0)[:, None]
    inverse = np.concatenate([cosine * multiplicity, -2.0 * sine])
    inverse[half] = alternating
    inverse = (inverse / (STEPS * weight)).T
    beta = wrap_factor ** (1.0 / STEPS)
    theta = 2.0 * np.pi * k / STEPS
    shift_one = 1.0 - beta * np.cos(theta)
    shift_two = shift_one.copy()
    shift_two[0] = 1.0 + beta
    coupling = beta * np.sin(theta)
    coupling[0] = 0.0
    wide = [np.repeat(v[:, None], 128, axis=1) for v in (shift_one, shift_two, coupling)]
    shifts = np.concatenate(wide).astype(np.float32)

    def parts(matrix):
        whole = matrix.astype(np.float32)
        high = whole.astype(jnp.bfloat16)
        low = (whole - high.astype(np.float32)).astype(jnp.bfloat16)
        return [high, low]

    select = np.zeros((DEPTH * 128, 256), np.float32)
    for row in range(ROWS):
        g, s = divmod(row + HALO, DEPTH)
        for c in range(TILE):
            select[128 * s + SPAN * g + HALO + c, 128 * (row // 16) + 8 * (row % 16) + c] = 1.0
    matrices = np.concatenate(parts(forward) + parts(inverse))
    return shifts, matrices, select.astype(jnp.bfloat16)


def residual_pack_send(me, y, row_slab, it, src, prv, cnd, res, out, inc, sems, local_sem):
    lane = lax.broadcasted_iota(jnp.int32, (8, 128), 1)
    column = lax.broadcasted_iota(jnp.int32, (FRAME, COLS), 1)
    field = it[...]
    left = jnp.where(column == 0, 0.0, pltpu.roll(field, 1, 1))
    right = jnp.where(column == COLS - 1, 0.0, pltpu.roll(field, COLS - 1, 1))
    lap = 4.0 * field - pltpu.roll(field, 1, 0) - pltpu.roll(field, FRAME - 1, 0) - left - right
    operated = cnd[:, 128 : 128 + COLS] * lap
    res[:, 128 : 128 + COLS] = src[...] - (field + time_step * operated - prv[...])
    zero = jnp.zeros((FRAME, 128), jnp.float32)
    for ref in (res, cnd):
        ref[:, :128] = zero
        ref[:, 128 + COLS :] = zero

    def send_tile(t, jj):
        peer = 16 * t + jj
        src_ref = out.at[pl.ds(pl.multiple_of(8 * peer, 8), DEPTH)]
        dst_ref = inc.at[pl.ds(pl.multiple_of(8 * me, 8), DEPTH)]

        @pl.when(peer != me)
        def _():
            pltpu.make_async_remote_copy(
                src_ref, dst_ref, sems.at[0], sems.at[1], device_id={"tm": peer}, device_id_type=MESH
            ).start()

        @pl.when(peer == me)
        def _():
            pltpu.make_async_copy(src_ref, dst_ref, local_sem).start()

    @pl.loop(0, 8)
    def _(i):
        half = (i + 1) // 2
        t = (y + 4 + jnp.where(i % 2 == 0, half, -half) + 8) % 8
        strips = []
        for g in range(GROUPS):
            rows = pl.ds(TOP + DEPTH * g, 8)
            strips.append(
                [res[rows, pl.ds(pl.multiple_of(128 * t + 128 * d, 128), 128)] for d in range(3)]
            )
        for jj in range(16):
            message = jnp.zeros((8, 128), jnp.float32)
            for g in range(GROUPS):
                before, strip, after = strips[g]
                if jj == 0:
                    strip = jnp.where(lane >= 64, before, strip)
                if jj == 15:
                    strip = jnp.where(lane < 64, after, strip)
                piece = pltpu.roll(strip, (SPAN * g - TILE * jj + HALO) % 128, 1)
                message = jnp.where((lane >= SPAN * g) & (lane < SPAN * (g + 1)), piece, message)
            out[pl.ds(pl.multiple_of(128 * t + 8 * jj, 8), 8)] = message
        for jj in range(16):
            send_tile(t, jj)


def own_conductivity(me, y, cnd):
    lane = lax.broadcasted_iota(jnp.int32, (8, 128), 1)
    jj = me % 16
    packed = jnp.zeros((8, 128), jnp.float32)
    for g in range(GROUPS):
        rows = pl.ds(TOP + DEPTH * g, 8)
        before, strip, after = [
            cnd[rows, pl.ds(pl.multiple_of(128 * y + 128 * d, 128), 128)] for d in range(3)
        ]
        strip = jnp.where((jj == 0) & (lane >= 64), before, strip)
        strip = jnp.where((jj == 15) & (lane < 64), after, strip)
        amount = (SPAN * g - TILE * jj + HALO + 128) % 128
        piece = pltpu.roll(strip, amount, 1)
        packed = jnp.where((lane >= SPAN * g) & (lane < SPAN * (g + 1)), piece, packed)
    return packed


def split(value):
    high = value.astype(jnp.bfloat16)
    return high, (value - high.astype(jnp.float32)).astype(jnp.bfloat16)


def dot(a, b):
    return jnp.dot(a, b, preferred_element_type=jnp.float32)


def transform(matrices, offset, high, low):
    table_high = matrices[offset : offset + 128]
    table_low = matrices[offset + 128 : offset + 256]
    return dot(table_high, high) + (dot(table_high, low) + dot(table_low, high))


def solve(packed, inc, spec, shifts, matrices, select, out):
    points = jnp.concatenate(
        [inc[pl.ds(s, STEPS, stride=8), :] for s in range(DEPTH)], axis=1
    )
    spec[...] = transform(matrices, 0, *split(points))
    diffusion = [
        jnp.broadcast_to(time_step * packed[s : s + 1, :], (8, 128)) for s in range(DEPTH)
    ]
    weights = sweep_weights(SWEEPS)

    @pl.loop(0, 8)
    def _(i):
        real = pl.ds(pl.multiple_of(8 * i, 8), 8)
        imag = pl.ds(pl.multiple_of(8 * i + 64, 8), 8)
        couple = pl.ds(pl.multiple_of(8 * i + 128, 8), 8)
        one, two, b = shifts[real, :], shifts[imag, :], shifts[couple, :]
        cr, ci, g1, g2, gb = [], [], [], [], []
        for s in range(DEPTH):
            d = diffusion[s]
            p1, p2 = one + 4.0 * d, two + 4.0 * d
            inv = 1.0 / (p1 * p2 + b * b)
            q1, q2, qb = p2 * inv, p1 * inv, b * inv
            lanes = pl.ds(128 * s, 128)
            sr, si = spec[real, lanes], spec[imag, lanes]
            cr.append(q1 * sr + qb * si)
            ci.append(q2 * si - qb * sr)
            g1.append(q1 * d)
            g2.append(q2 * d)
            gb.append(qb * d)
        re = [weights[0] * v for v in cr]
        im = [weights[0] * v for v in ci]

        def neighbours(f):
            above = [pltpu.roll(f[DEPTH - 1], SPAN, 1)] + f[:-1]
            below = f[1:] + [pltpu.roll(f[0], 128 - SPAN, 1)]
            return [
                (above[s] + below[s]) + (pltpu.roll(f[s], 1, 1) + pltpu.roll(f[s], 127, 1))
                for s in range(DEPTH)
            ]

        for w in weights[1:]:
            nr, ni = neighbours(re), neighbours(im)
            re, im = (
                [
                    (1.0 - w) * re[s] + w * (cr[s] + g1[s] * nr[s] + gb[s] * ni[s])
                    for s in range(DEPTH)
                ],
                [
                    (1.0 - w) * im[s] + w * (ci[s] + g2[s] * ni[s] - gb[s] * nr[s])
                    for s in range(DEPTH)
                ],
            )
        for s in range(DEPTH):
            lanes = pl.ds(128 * s, 128)
            spec[real, lanes] = re[s]
            spec[imag, lanes] = im[s]

    high, low = split(spec[...])
    picked_high = dot(high, select[...]).astype(jnp.bfloat16)
    picked_low = dot(low, select[...]).astype(jnp.bfloat16)
    back = transform(matrices, 256, picked_high, picked_low)
    out[pl.ds(0, STEPS, stride=8), :] = back[:, :128]
    out[pl.ds(1, STEPS, stride=8), :] = back[:, 128:]


def main_kernel(
    src_in, it_in, ini_in, cnd_in, shifts_in, matrices_in, select_in,
    back_ref,
    it, src, prv, cnd, res, out, inc, spec, out2, shifts, matrices, select,
    send_sem, recv_sem, local_sem, table_sem, a2a_sem, a2a2_sem, self_sem,
):
    me = lax.axis_index("tm")
    slab = lax.axis_index("rows")
    y = me // 16
    after, before = (me + 1) % STEPS, (me + STEPS - 1) % STEPS
    down, up = (slab + 1) % 4, (slab + 3) % 4

    tables_in = [
        pltpu.make_async_copy(a, b, table_sem.at[i])
        for i, (a, b) in enumerate(
            [(shifts_in, shifts), (matrices_in, matrices), (select_in, select)]
        )
    ]
    inside = pl.ds(128, COLS)
    own = [
        pltpu.make_async_copy(it_in.at[0], it.at[pl.ds(8, ROWS)], local_sem.at[0]),
        pltpu.make_async_copy(src_in.at[0], src.at[pl.ds(8, ROWS)], local_sem.at[1]),
        pltpu.make_async_copy(cnd_in, cnd.at[pl.ds(8, ROWS), inside], local_sem.at[2]),
    ]
    for copy in own + tables_in:
        copy.start()

    barrier = pltpu.get_barrier_semaphore()
    for i in range(1, STEPS):
        pl.semaphore_signal(
            barrier, inc=1, device_id={"tm": (me + i) % STEPS}, device_id_type=MESH
        )
    greeted = [{"rows": down}, {"rows": up}]
    greeted += [{"tm": t, "rows": r} for t in (after, before) for r in (down, up)]
    for peer in greeted:
        pl.semaphore_signal(barrier, inc=1, device_id=peer, device_id_type=MESH)
    pl.semaphore_wait(barrier, STEPS - 1 + len(greeted))

    def remote(i, a, b, peer):
        return pltpu.make_async_remote_copy(
            a, b, send_sem.at[i], recv_sem.at[i], device_id=peer, device_id_type=MESH
        )

    def rows(ref, first, count):
        return ref.at[pl.ds(first, count)]

    it_own, src_own = it_in.at[0], src_in.at[0]

    def previous(value):
        return [
            remote(0, value, rows(prv, 8, ROWS), {"tm": after}),
            remote(1, rows(value, ROWS - HALO, HALO), rows(prv, TOP, HALO), {"tm": after, "rows": down}),
            remote(2, rows(value, 0, HALO), rows(prv, 8 + ROWS, HALO), {"tm": after, "rows": up}),
        ]

    @pl.when(me < STEPS - 1)
    def _():
        for copy in previous(it_own):
            copy.start()

    @pl.when(me == STEPS - 1)
    def _():
        for copy in previous(ini_in):
            copy.start()

    halos = [
        remote(3, rows(it_own, ROWS - HALO - 1, HALO + 1), rows(it, TOP - 1, HALO + 1), {"rows": down}),
        remote(4, rows(it_own, 0, HALO + 1), rows(it, 8 + ROWS, HALO + 1), {"rows": up}),
        remote(5, rows(src_own, ROWS - HALO, HALO), rows(src, TOP, HALO), {"rows": down}),
        remote(6, rows(src_own, 0, HALO), rows(src, 8 + ROWS, HALO), {"rows": up}),
        remote(7, rows(cnd_in, ROWS - HALO, HALO), cnd.at[pl.ds(TOP, HALO), inside], {"rows": down}),
        remote(8, rows(cnd_in, 0, HALO), cnd.at[pl.ds(8 + ROWS, HALO), inside], {"rows": up}),
    ]
    for copy in halos:
        copy.start()
    for copy in own:
        copy.wait()
    for copy in previous(ini_in) + halos:
        copy.wait()

    @pl.when(slab == 0)
    def _():
        for ref in (it, src, prv, cnd):
            ref[0:8, :] = jnp.zeros((8, ref.shape[1]), jnp.float32)

    @pl.when(slab == 3)
    def _():
        for ref in (it, src, prv, cnd):
            ref[8 + ROWS :, :] = jnp.zeros((8, ref.shape[1]), jnp.float32)

    residual_pack_send(me, y, slab, it, src, prv, cnd, res, out, inc, a2a_sem, self_sem.at[0])
    packed = own_conductivity(me, y, cnd)

    def wait_all(a, b, depth, sems, sem):
        share = (STEPS - 1) * depth
        pltpu.make_async_copy(rows(a, 0, depth), rows(b, 0, depth), sem).wait()
        pltpu.make_async_remote_copy(
            rows(a, 0, share), rows(b, 0, share), sems.at[0], sems.at[1],
            device_id={"tm": after}, device_id_type=MESH,
        ).wait()

    for copy in tables_in:
        copy.wait()
    wait_all(out, inc, DEPTH, a2a_sem, self_sem.at[0])
    solve(packed, inc, spec, shifts, matrices, select, out2)

    mine = pl.ds(pl.multiple_of(8 * me, 8), 2)
    pltpu.make_async_copy(out2.at[mine], back_ref.at[mine], self_sem.at[1]).start()

    @pl.loop(1, STEPS)
    def _(i):
        peer = (me + i) % STEPS
        pltpu.make_async_remote_copy(
            out2.at[pl.ds(pl.multiple_of(8 * peer, 8), 2)], back_ref.at[mine],
            a2a2_sem.at[0], a2a2_sem.at[1], device_id={"tm": peer}, device_id_type=MESH,
        ).start()

    wait_all(out2, back_ref, 2, a2a2_sem, self_sem.at[1])


def unpack_kernel(back, out):
    block = lax.broadcasted_iota(jnp.int32, (128, 128), 1) // 8
    tile = lax.broadcasted_iota(jnp.int32, (128, 128), 0)
    for h in range(2):
        x = back[pl.ds(h, 128, stride=8), :]
        for bit in (1, 2, 4, 8):
            lane_set, tile_set = (block & bit) != 0, (tile & bit) != 0
            from_next = pltpu.roll(pltpu.roll(x, 128 - bit, 0), 8 * bit, 1)
            from_last = pltpu.roll(pltpu.roll(x, bit, 0), 128 - 8 * bit, 1)
            moved = jnp.where(lane_set, from_next, from_last)
            x = jnp.where(lane_set == tile_set, x, moved)
        for t in range(8):
            out[0, 16 * h : 16 * h + 16, 128 * t : 128 * t + 128] = x[16 * t : 16 * t + 16]


def shards(source_term, iterate, initial, conductivity):
    shifts, matrices, select = tables()
    f32 = jnp.float32
    dma = pltpu.SemaphoreType.DMA
    back = pl.pallas_call(
        main_kernel,
        out_shape=jax.ShapeDtypeStruct((1024, 128), f32),
        in_specs=[pl.BlockSpec(memory_space=pl.ANY)] * 7,
        out_specs=pl.BlockSpec(memory_space=pl.ANY),
        scratch_shapes=[
            pltpu.VMEM((FRAME, COLS), f32),
            pltpu.VMEM((FRAME, COLS), f32),
            pltpu.VMEM((FRAME, COLS), f32),
            pltpu.VMEM((FRAME, COLS + 256), f32),
            pltpu.VMEM((FRAME, COLS + 256), f32),
            pltpu.VMEM((1024, 128), f32),
            pltpu.VMEM((1024, 128), f32),
            pltpu.VMEM((128, DEPTH * 128), f32),
            pltpu.VMEM((1024, 128), f32),
            pltpu.VMEM(shifts.shape, f32),
            pltpu.VMEM(matrices.shape, jnp.bfloat16),
            pltpu.VMEM(select.shape, jnp.bfloat16),
            dma((9,)), dma((9,)), dma((3,)), dma((3,)), dma((2,)), dma((2,)), dma((2,)),
        ],
        compiler_params=pltpu.CompilerParams(collective_id=0, has_side_effects=True),
        name="main",
    )(source_term, iterate, initial, conductivity, shifts, matrices, select)
    return pl.pallas_call(
        unpack_kernel,
        out_shape=jax.ShapeDtypeStruct((1, ROWS, COLS), f32),
        in_specs=[pl.BlockSpec(memory_space=pltpu.VMEM)],
        out_specs=pl.BlockSpec(memory_space=pltpu.VMEM),
        name="unpack",
    )(back)


def solution(mesh):
    in_specs = (P("tm", "rows", None), P("tm", "rows", None), P("rows", None), P("rows", None))
    out_specs = P("tm", "rows", None)
    return jax.shard_map(shards, mesh=mesh, in_specs=in_specs, out_specs=out_specs, check_vma=False)
```

```python
import functools
import math

import jax
import jax.numpy as jnp
import numpy as np
from jax import lax
from jax.experimental import pallas as pl
from jax.experimental.pallas import tpu as pltpu
from jax.sharding import PartitionSpec as P

MESH = pl.DeviceIdType.MESH

SWEEPS = 6
time_step = 0.5
wrap_factor = 0.25
chebyshev_spread = 0.7

STEPS = 128
COLS = 1024
ROWS = 32
TILE = 8
HALO = SWEEPS - 1
COLLECT_LOW = 16 * 5 + 2 * 2
COLLECT_ALL = 16 * 5 + 2 * 5
BLOCK = 32
FAR_ROWS = (4, 3, 5, 2, 6, 1, 7, 0)
FAR_FIRST = sorted(
    [(dy, dz, dc) for dy in range(8) for dz in range(8) for dc in range(2) if dy or dz or dc],
    key=lambda d: -min(d[0], 8 - d[0]) - min(d[1], 8 - d[1]),
)
SPAN = TILE + 2 * HALO
GROUPS = 7
DEPTH = 6
TOP = 8 - HALO
FRAME = ROWS + 16


def sweep_weights(count):
    return [
        1.0 / (1.0 + chebyshev_spread * math.cos(math.pi * (2 * sweep + 1) / (2 * count)))
        for sweep in range(count)
    ]


def tables():
    half = STEPS // 2
    k = np.arange(half)
    n = np.arange(STEPS)
    angle = 2.0 * np.pi * (k[:, None] * n[None, :] % STEPS) / STEPS
    weight = wrap_factor ** (n / STEPS)
    cosine, sine = np.cos(angle), np.sin(angle)
    alternating = np.where(n % 2 == 0, 1.0, -1.0)
    forward = np.concatenate([cosine, -sine]) * weight
    forward[half] = alternating * weight
    multiplicity = np.where(k == 0, 1.0, 2.0)[:, None]
    inverse = np.concatenate([cosine * multiplicity, -2.0 * sine])
    inverse[half] = alternating
    inverse = (inverse / (STEPS * weight)).T
    beta = wrap_factor ** (1.0 / STEPS)
    theta = 2.0 * np.pi * k / STEPS
    shift_one = 1.0 - beta * np.cos(theta)
    shift_two = shift_one.copy()
    shift_two[0] = 1.0 + beta
    coupling = beta * np.sin(theta)
    coupling[0] = 0.0
    wide = [np.repeat(v[:, None], 128, axis=1) for v in (shift_one, shift_two, coupling)]
    shifts = np.concatenate(wide).astype(np.float32)

    def parts(matrix):
        whole = matrix.astype(np.float32)
        high = whole.astype(jnp.bfloat16)
        low = (whole - high.astype(np.float32)).astype(jnp.bfloat16)
        return [high, low]

    select = np.zeros((DEPTH * 128, 256), np.float32)
    for row in range(ROWS):
        g, s = divmod(row + HALO, DEPTH)
        for c in range(TILE):
            select[128 * s + SPAN * g + HALO + c, 128 * (row // 16) + 8 * (row % 16) + c] = 1.0
    matrices = np.concatenate(parts(forward) + parts(inverse))
    return shifts, matrices, select.astype(jnp.bfloat16)


def residual_pack_send(me, y, z, core, it, src, prv, cnd, res, out, inc, sems, local_sem, ready):
    lane = lax.broadcasted_iota(jnp.int32, (8, 128), 1)
    column = lax.broadcasted_iota(jnp.int32, (FRAME, COLS), 1)
    field = it[...]
    left = jnp.where(column == 0, 0.0, pltpu.roll(field, 1, 1))
    right = jnp.where(column == COLS - 1, 0.0, pltpu.roll(field, COLS - 1, 1))
    lap = 4.0 * field - pltpu.roll(field, 1, 0) - pltpu.roll(field, FRAME - 1, 0) - left - right
    operated = cnd[:, 128 : 128 + COLS] * lap
    res[:, 128 : 128 + COLS] = src[...] - (field + time_step * operated - prv[...])
    zero = jnp.zeros((FRAME, 128), jnp.float32)
    for ref in (res, cnd):
        ref[:, :128] = zero
        ref[:, 128 + COLS :] = zero

    def send(peer):
        pltpu.make_async_remote_copy(
            out.at[pl.ds(pl.multiple_of(8 * peer, 8), DEPTH)],
            inc.at[pl.ds(pl.multiple_of(8 * me, 8), DEPTH)],
            sems.at[0], sems.at[1], device_id={"tm": peer}, device_id_type=MESH,
        ).start()

    pl.semaphore_wait(ready.at[z // 4], 1)
    low = z < 4

    @pl.loop(0, 8)
    def _(i):
        half = (i + 1) // 2
        t = (y + 4 + jnp.where(i % 2 == 0, half, -half) + 8) % 8
        plain, first, last = [], [], []
        for g in range(GROUPS):
            rows = pl.ds(TOP + DEPTH * g, 8)
            before, strip, after = [
                res[rows, pl.ds(pl.multiple_of(128 * t + 128 * d, 128), 128)] for d in range(3)
            ]
            amount = SPAN * g + HALO
            plain.append(pltpu.roll(strip, amount, 1))
            first.append(pltpu.roll(jnp.where(lane >= 64, before, strip), amount, 1))
            last.append(pltpu.roll(jnp.where(lane < 64, after, strip), amount, 1))
        for jj in range(16):
            strips = first if jj == 0 else last if jj == 15 else plain
            place = (lane + (128 - TILE * jj)) % 128
            message = strips[0]
            for g in range(1, GROUPS):
                message = jnp.where(place >= SPAN * g, strips[g], message)
            out[pl.ds(pl.multiple_of(128 * t + 8 * jj, 8), 8)] = pltpu.roll(
                message, (128 - TILE * jj) % 128, 1
            )
        for turn in range(1, 4):
            for c in range(2):
                send(16 * t + 2 * (z // 4 * 4 + (z + turn) % 4) + c)
        send(16 * t + 2 * z + 1 - core)

        @pl.when(t != y)
        def _():
            send(16 * t + 2 * z + core)

        @pl.when(jnp.logical_not(low))
        def _():
            for plane in range(4):
                for c in range(2):
                    send(16 * t + 2 * plane + c)

    mine = pl.ds(pl.multiple_of(8 * me, 8), DEPTH)
    pltpu.make_async_copy(out.at[mine], inc.at[mine], local_sem).start()

    @pl.when(low)
    def _():
        pl.semaphore_wait(ready.at[1], 1)

        @pl.loop(0, 8)
        def _(i):
            half = (i + 1) // 2
            t = (y + 4 + jnp.where(i % 2 == 0, half, -half) + 8) % 8
            for plane in range(4, 8):
                for c in range(2):
                    send(16 * t + 2 * plane + c)


def own_conductivity(me, y, cnd):
    lane = lax.broadcasted_iota(jnp.int32, (8, 128), 1)
    jj = me % 16
    packed = jnp.zeros((8, 128), jnp.float32)
    for g in range(GROUPS):
        rows = pl.ds(TOP + DEPTH * g, 8)
        before, strip, after = [
            cnd[rows, pl.ds(pl.multiple_of(128 * y + 128 * d, 128), 128)] for d in range(3)
        ]
        strip = jnp.where((jj == 0) & (lane >= 64), before, strip)
        strip = jnp.where((jj == 15) & (lane < 64), after, strip)
        amount = (SPAN * g - TILE * jj + HALO + 128) % 128
        piece = pltpu.roll(strip, amount, 1)
        packed = jnp.where((lane >= SPAN * g) & (lane < SPAN * (g + 1)), piece, packed)
    return packed


def split(value):
    high = value.astype(jnp.bfloat16)
    return high, (value - high.astype(jnp.float32)).astype(jnp.bfloat16)


def dot(a, b):
    return jnp.dot(a, b, preferred_element_type=jnp.float32)


def transform(matrices, offset, high, low):
    table_high = matrices[offset : offset + 128]
    table_low = matrices[offset + 128 : offset + 256]
    return dot(table_high, high) + (dot(table_high, low) + dot(table_low, high))


def solve(packed, inc, spec, shifts, matrices, select, out):
    points = jnp.concatenate(
        [inc[pl.ds(s, STEPS, stride=8), :] for s in range(DEPTH)], axis=1
    )
    spec[...] = transform(matrices, 0, *split(points))
    diffusion = [
        jnp.broadcast_to(time_step * packed[s : s + 1, :], (BLOCK, 128)) for s in range(DEPTH)
    ]
    weights = sweep_weights(SWEEPS)

    @pl.loop(0, 64 // BLOCK)
    def _(i):
        real = pl.ds(pl.multiple_of(BLOCK * i, BLOCK), BLOCK)
        imag = pl.ds(pl.multiple_of(BLOCK * i + 64, BLOCK), BLOCK)
        couple = pl.ds(pl.multiple_of(BLOCK * i + 128, BLOCK), BLOCK)
        one, two, b = shifts[real, :], shifts[imag, :], shifts[couple, :]
        cr, ci, g1, g2, gb = [], [], [], [], []
        for s in range(DEPTH):
            d = diffusion[s]
            p1, p2 = one + 4.0 * d, two + 4.0 * d
            inv = 1.0 / (p1 * p2 + b * b)
            q1, q2, qb = p2 * inv, p1 * inv, b * inv
            lanes = pl.ds(128 * s, 128)
            sr, si = spec[real, lanes], spec[imag, lanes]
            cr.append(q1 * sr + qb * si)
            ci.append(q2 * si - qb * sr)
            g1.append(q1 * d)
            g2.append(q2 * d)
            gb.append(qb * d)
        re = [weights[0] * v for v in cr]
        im = [weights[0] * v for v in ci]

        def neighbours(f):
            above = [pltpu.roll(f[DEPTH - 1], SPAN, 1)] + f[:-1]
            below = f[1:] + [pltpu.roll(f[0], 128 - SPAN, 1)]
            return [
                (above[s] + below[s]) + (pltpu.roll(f[s], 1, 1) + pltpu.roll(f[s], 127, 1))
                for s in range(DEPTH)
            ]

        for w in weights[1:]:
            nr, ni = neighbours(re), neighbours(im)
            re, im = (
                [
                    (1.0 - w) * re[s] + w * (cr[s] + g1[s] * nr[s] + gb[s] * ni[s])
                    for s in range(DEPTH)
                ],
                [
                    (1.0 - w) * im[s] + w * (ci[s] + g2[s] * ni[s] - gb[s] * nr[s])
                    for s in range(DEPTH)
                ],
            )
        for s in range(DEPTH):
            lanes = pl.ds(128 * s, 128)
            spec[real, lanes] = re[s]
            spec[imag, lanes] = im[s]

    high, low = split(spec[...])
    picked_high = dot(high, select[...]).astype(jnp.bfloat16)
    picked_low = dot(low, select[...]).astype(jnp.bfloat16)
    back = transform(matrices, 256, picked_high, picked_low)
    out[pl.ds(0, STEPS, stride=8), :] = back[:, :128]
    out[pl.ds(1, STEPS, stride=8), :] = back[:, 128:]


def main_kernel(
    src_in, it_in, ini_in, cnd_in, shifts_in, matrices_in, select_in,
    back_ref,
    it, src, prv, cnd, res, out, inc, spec, out2, shifts, matrices, select,
    send_sem, recv_sem, local_sem, table_sem, a2a_sem, a2a2_sem, self_sem, ready,
):
    me = lax.axis_index("tm")
    slab = lax.axis_index("rows")
    y, z, core = me // 16, me // 2 % 8, me % 2
    after, before = (me + 1) % STEPS, (me + STEPS - 1) % STEPS
    down, up = (slab + 1) % 4, (slab + 3) % 4

    tables_in = [
        pltpu.make_async_copy(a, b, table_sem.at[i])
        for i, (a, b) in enumerate(
            [(shifts_in, shifts), (matrices_in, matrices), (select_in, select)]
        )
    ]
    inside = pl.ds(128, COLS)
    own = [
        pltpu.make_async_copy(it_in.at[0], it.at[pl.ds(8, ROWS)], local_sem.at[0]),
        pltpu.make_async_copy(src_in.at[0], src.at[pl.ds(8, ROWS)], local_sem.at[1]),
        pltpu.make_async_copy(cnd_in, cnd.at[pl.ds(8, ROWS), inside], local_sem.at[2]),
    ]
    for copy in own + tables_in:
        copy.start()

    barrier = pltpu.get_barrier_semaphore()

    def tell(sem, peer):
        pl.semaphore_signal(sem, inc=1, device_id=peer, device_id_type=MESH)

    greeted = [{"tm": after}, {"tm": before}, {"rows": down}, {"rows": up}]
    greeted += [{"tm": t, "rows": r} for t in (after, before) for r in (down, up)]
    for peer in greeted:
        tell(barrier, peer)
    low = z < 4
    for c in range(2):
        for collector, when in ((COLLECT_LOW + c, low), (COLLECT_ALL + c, True)):

            @pl.when(jnp.logical_and(me != collector, when))
            def _():
                tell(barrier, {"tm": collector})

    collects_low, collects_all = me // 2 == COLLECT_LOW // 2, me // 2 == COLLECT_ALL // 2
    heard = jnp.where(collects_low, STEPS // 2 - 1, 0) + jnp.where(collects_all, STEPS - 1, 0)
    pl.semaphore_wait(barrier, len(greeted) + heard)

    @pl.when(collects_low)
    def _():
        for dy in range(8):
            for plane in range(4):
                if 16 * dy + 2 * plane != COLLECT_LOW:
                    tell(ready.at[0], {"tm": 16 * dy + 2 * plane + core})
        pl.semaphore_signal(ready.at[0], inc=1)

    @pl.when(collects_all)
    def _():
        for dy, dz, dc in FAR_FIRST:
            if dc == 0:
                tell(ready.at[1], {"tm": (y + dy) % 8 * 16 + (z + dz) % 8 * 2 + core})
        pl.semaphore_signal(ready.at[1], inc=1)

    def remote(i, a, b, peer):
        return pltpu.make_async_remote_copy(
            a, b, send_sem.at[i], recv_sem.at[i], device_id=peer, device_id_type=MESH
        )

    def rows(ref, first, count):
        return ref.at[pl.ds(first, count)]

    it_own, src_own = it_in.at[0], src_in.at[0]

    def previous(value):
        return [
            remote(0, value, rows(prv, 8, ROWS), {"tm": after}),
            remote(1, rows(value, ROWS - HALO, HALO), rows(prv, TOP, HALO), {"tm": after, "rows": down}),
            remote(2, rows(value, 0, HALO), rows(prv, 8 + ROWS, HALO), {"tm": after, "rows": up}),
        ]

    @pl.when(me < STEPS - 1)
    def _():
        for copy in previous(it_own):
            copy.start()

    @pl.when(me == STEPS - 1)
    def _():
        for copy in previous(ini_in):
            copy.start()

    halos = [
        remote(3, rows(it_own, ROWS - HALO - 1, HALO + 1), rows(it, TOP - 1, HALO + 1), {"rows": down}),
        remote(4, rows(it_own, 0, HALO + 1), rows(it, 8 + ROWS, HALO + 1), {"rows": up}),
        remote(5, rows(src_own, ROWS - HALO, HALO), rows(src, TOP, HALO), {"rows": down}),
        remote(6, rows(src_own, 0, HALO), rows(src, 8 + ROWS, HALO), {"rows": up}),
        remote(7, rows(cnd_in, ROWS - HALO, HALO), cnd.at[pl.ds(TOP, HALO), inside], {"rows": down}),
        remote(8, rows(cnd_in, 0, HALO), cnd.at[pl.ds(8 + ROWS, HALO), inside], {"rows": up}),
    ]
    for copy in halos:
        copy.start()
    for copy in own:
        copy.wait()
    for copy in previous(ini_in) + halos:
        copy.wait()

    @pl.when(slab == 0)
    def _():
        for ref in (it, src, prv, cnd):
            ref[0:8, :] = jnp.zeros((8, ref.shape[1]), jnp.float32)

    @pl.when(slab == 3)
    def _():
        for ref in (it, src, prv, cnd):
            ref[8 + ROWS :, :] = jnp.zeros((8, ref.shape[1]), jnp.float32)

    residual_pack_send(me, y, z, core, it, src, prv, cnd, res, out, inc, a2a_sem, self_sem.at[0], ready)
    packed = own_conductivity(me, y, cnd)

    def wait_all(a, b, depth, sems, sem):
        share = (STEPS - 1) * depth
        pltpu.make_async_copy(rows(a, 0, depth), rows(b, 0, depth), sem).wait()
        pltpu.make_async_remote_copy(
            rows(a, 0, share), rows(b, 0, share), sems.at[0], sems.at[1],
            device_id={"tm": after}, device_id_type=MESH,
        ).wait()

    for copy in tables_in:
        copy.wait()
    wait_all(out, inc, DEPTH, a2a_sem, self_sem.at[0])
    solve(packed, inc, spec, shifts, matrices, select, out2)

    mine = pl.ds(pl.multiple_of(8 * me, 8), 2)
    pltpu.make_async_copy(out2.at[mine], back_ref.at[mine], self_sem.at[1]).start()

    for dy, dz, dc in FAR_FIRST:
        peer = (y + dy) % 8 * 16 + (z + dz) % 8 * 2 + (core + dc) % 2
        pltpu.make_async_remote_copy(
            out2.at[pl.ds(pl.multiple_of(8 * peer, 8), 2)], back_ref.at[mine],
            a2a2_sem.at[0], a2a2_sem.at[1], device_id={"tm": peer}, device_id_type=MESH,
        ).start()

    wait_all(out2, back_ref, 2, a2a2_sem, self_sem.at[1])


def unpack_kernel(back, out):
    block = lax.broadcasted_iota(jnp.int32, (128, 128), 1) // 8
    tile = lax.broadcasted_iota(jnp.int32, (128, 128), 0)
    for h in range(2):
        x = back[pl.ds(h, 128, stride=8), :]
        for bit in (1, 2, 4, 8):
            lane_set, tile_set = (block & bit) != 0, (tile & bit) != 0
            from_next = pltpu.roll(pltpu.roll(x, 128 - bit, 0), 8 * bit, 1)
            from_last = pltpu.roll(pltpu.roll(x, bit, 0), 128 - 8 * bit, 1)
            moved = jnp.where(lane_set, from_next, from_last)
            x = jnp.where(lane_set == tile_set, x, moved)
        for t in range(8):
            out[0, 16 * h : 16 * h + 16, 128 * t : 128 * t + 128] = x[16 * t : 16 * t + 16]


def shards(source_term, iterate, initial, conductivity):
    shifts, matrices, select = tables()
    f32 = jnp.float32
    dma = pltpu.SemaphoreType.DMA
    back = pl.pallas_call(
        main_kernel,
        out_shape=jax.ShapeDtypeStruct((1024, 128), f32),
        in_specs=[pl.BlockSpec(memory_space=pl.ANY)] * 7,
        out_specs=pl.BlockSpec(memory_space=pl.ANY),
        scratch_shapes=[
            pltpu.VMEM((FRAME, COLS), f32),
            pltpu.VMEM((FRAME, COLS), f32),
            pltpu.VMEM((FRAME, COLS), f32),
            pltpu.VMEM((FRAME, COLS + 256), f32),
            pltpu.VMEM((FRAME, COLS + 256), f32),
            pltpu.VMEM((1024, 128), f32),
            pltpu.VMEM((1024, 128), f32),
            pltpu.VMEM((128, DEPTH * 128), f32),
            pltpu.VMEM((1024, 128), f32),
            pltpu.VMEM(shifts.shape, f32),
            pltpu.VMEM(matrices.shape, jnp.bfloat16),
            pltpu.VMEM(select.shape, jnp.bfloat16),
            dma((9,)), dma((9,)), dma((3,)), dma((3,)), dma((2,)), dma((2,)), dma((2,)),
            pltpu.SemaphoreType.REGULAR((2,)),
        ],
        compiler_params=pltpu.CompilerParams(collective_id=0, has_side_effects=True),
        name="main",
    )(source_term, iterate, initial, conductivity, shifts, matrices, select)
    return pl.pallas_call(
        unpack_kernel,
        out_shape=jax.ShapeDtypeStruct((1, ROWS, COLS), f32),
        in_specs=[pl.BlockSpec(memory_space=pltpu.VMEM)],
        out_specs=pl.BlockSpec(memory_space=pltpu.VMEM),
        name="unpack",
    )(back)


def solution(mesh):
    in_specs = (P("tm", "rows", None), P("tm", "rows", None), P("rows", None), P("rows", None))
    out_specs = P("tm", "rows", None)
    return jax.shard_map(shards, mesh=mesh, in_specs=in_specs, out_specs=out_specs, check_vma=False)
```

```python
import functools
import math

import jax
import jax.numpy as jnp
import numpy as np
from jax import lax
from jax.experimental import pallas as pl
from jax.experimental.pallas import tpu as pltpu
from jax.sharding import PartitionSpec as P

MESH = pl.DeviceIdType.MESH

SWEEPS = 6
time_step = 0.5
wrap_factor = 0.25
chebyshev_spread = 0.7

STEPS = 128
COLS = 1024
ROWS = 32
TILE = 8
HALO = SWEEPS - 1
COLLECT_LOW = 16 * 5 + 2 * 2
COLLECT_ALL = 16 * 5 + 2 * 5
FAR_ROWS = (4, 3, 5, 2, 6, 1, 7, 0)
FAR_FIRST = sorted(
    [(dy, dz, dc) for dy in range(8) for dz in range(8) for dc in range(2) if dy or dz or dc],
    key=lambda d: -min(d[0], 8 - d[0]) - min(d[1], 8 - d[1]),
)
SPAN = TILE + 2 * HALO
GROUPS = 7
DEPTH = 6
TOP = 8 - HALO
FRAME = ROWS + 16


def sweep_weights(count):
    return [
        1.0 / (1.0 + chebyshev_spread * math.cos(math.pi * (2 * sweep + 1) / (2 * count)))
        for sweep in range(count)
    ]


def tables():
    half = STEPS // 2
    k = np.arange(half)
    n = np.arange(STEPS)
    angle = 2.0 * np.pi * (k[:, None] * n[None, :] % STEPS) / STEPS
    weight = wrap_factor ** (n / STEPS)
    cosine, sine = np.cos(angle), np.sin(angle)
    alternating = np.where(n % 2 == 0, 1.0, -1.0)
    forward = np.concatenate([cosine, -sine]) * weight
    forward[half] = alternating * weight
    multiplicity = np.where(k == 0, 1.0, 2.0)[:, None]
    inverse = np.concatenate([cosine * multiplicity, -2.0 * sine])
    inverse[half] = alternating
    inverse = (inverse / (STEPS * weight)).T
    beta = wrap_factor ** (1.0 / STEPS)
    theta = 2.0 * np.pi * k / STEPS
    shift_one = 1.0 - beta * np.cos(theta)
    shift_two = shift_one.copy()
    shift_two[0] = 1.0 + beta
    coupling = beta * np.sin(theta)
    coupling[0] = 0.0
    wide = [np.repeat(v[:, None], 128, axis=1) for v in (shift_one, shift_two, coupling)]
    shifts = np.concatenate(wide).astype(np.float32)

    def parts(matrix):
        whole = matrix.astype(np.float32)
        high = whole.astype(jnp.bfloat16)
        low = (whole - high.astype(np.float32)).astype(jnp.bfloat16)
        return [high, low]

    select = np.zeros((DEPTH * 128, 256), np.float32)
    for row in range(ROWS):
        g, s = divmod(row + HALO, DEPTH)
        for c in range(TILE):
            select[128 * s + SPAN * g + HALO + c, 128 * (row // 16) + 8 * (row % 16) + c] = 1.0
    matrices = np.concatenate(parts(forward) + parts(inverse))
    return shifts, matrices, select.astype(jnp.bfloat16)


def residual_pack_send(me, y, z, core, it, src, prv, cnd, res, out, inc, sems, local_sem, ready):
    lane = lax.broadcasted_iota(jnp.int32, (8, 128), 1)
    column = lax.broadcasted_iota(jnp.int32, (FRAME, COLS), 1)
    field = it[...]
    left = jnp.where(column == 0, 0.0, pltpu.roll(field, 1, 1))
    right = jnp.where(column == COLS - 1, 0.0, pltpu.roll(field, COLS - 1, 1))
    lap = 4.0 * field - pltpu.roll(field, 1, 0) - pltpu.roll(field, FRAME - 1, 0) - left - right
    operated = cnd[:, 128 : 128 + COLS] * lap
    res[:, 128 : 128 + COLS] = src[...] - (field + time_step * operated - prv[...])
    zero = jnp.zeros((FRAME, 128), jnp.float32)
    for ref in (res, cnd):
        ref[:, :128] = zero
        ref[:, 128 + COLS :] = zero

    def send(peer):
        pltpu.make_async_remote_copy(
            out.at[pl.ds(pl.multiple_of(8 * peer, 8), DEPTH)],
            inc.at[pl.ds(pl.multiple_of(8 * me, 8), DEPTH)],
            sems.at[0], sems.at[1], device_id={"tm": peer}, device_id_type=MESH,
        ).start()

    pl.semaphore_wait(ready.at[z // 4], 1)
    low = z < 4

    @pl.loop(0, 8)
    def _(i):
        half = (i + 1) // 2
        t = (y + 4 + jnp.where(i % 2 == 0, half, -half) + 8) % 8
        plain, first, last = [], [], []
        for g in range(GROUPS):
            rows = pl.ds(TOP + DEPTH * g, 8)
            before, strip, after = [
                res[rows, pl.ds(pl.multiple_of(128 * t + 128 * d, 128), 128)] for d in range(3)
            ]
            amount = SPAN * g + HALO
            plain.append(pltpu.roll(strip, amount, 1))
            first.append(pltpu.roll(jnp.where(lane >= 64, before, strip), amount, 1))
            last.append(pltpu.roll(jnp.where(lane < 64, after, strip), amount, 1))
        for jj in range(16):
            strips = first if jj == 0 else last if jj == 15 else plain
            place = (lane + (128 - TILE * jj)) % 128
            message = strips[0]
            for g in range(1, GROUPS):
                message = jnp.where(place >= SPAN * g, strips[g], message)
            out[pl.ds(pl.multiple_of(128 * t + 8 * jj, 8), 8)] = pltpu.roll(
                message, (128 - TILE * jj) % 128, 1
            )
        for turn in range(1, 4):
            for c in range(2):
                send(16 * t + 2 * (z // 4 * 4 + (z + turn) % 4) + c)
        send(16 * t + 2 * z + 1 - core)

        @pl.when(t != y)
        def _():
            send(16 * t + 2 * z + core)

        @pl.when(jnp.logical_not(low))
        def _():
            for plane in range(4):
                for c in range(2):
                    send(16 * t + 2 * plane + c)

    mine = pl.ds(pl.multiple_of(8 * me, 8), DEPTH)
    pltpu.make_async_copy(out.at[mine], inc.at[mine], local_sem).start()

    @pl.when(low)
    def _():
        pl.semaphore_wait(ready.at[1], 1)

        @pl.loop(0, 8)
        def _(i):
            half = (i + 1) // 2
            t = (y + 4 + jnp.where(i % 2 == 0, half, -half) + 8) % 8
            for plane in range(4, 8):
                for c in range(2):
                    send(16 * t + 2 * plane + c)


def own_conductivity(me, y, cnd):
    lane = lax.broadcasted_iota(jnp.int32, (8, 128), 1)
    jj = me % 16
    packed = jnp.zeros((8, 128), jnp.float32)
    for g in range(GROUPS):
        rows = pl.ds(TOP + DEPTH * g, 8)
        before, strip, after = [
            cnd[rows, pl.ds(pl.multiple_of(128 * y + 128 * d, 128), 128)] for d in range(3)
        ]
        strip = jnp.where((jj == 0) & (lane >= 64), before, strip)
        strip = jnp.where((jj == 15) & (lane < 64), after, strip)
        amount = (SPAN * g - TILE * jj + HALO + 128) % 128
        piece = pltpu.roll(strip, amount, 1)
        packed = jnp.where((lane >= SPAN * g) & (lane < SPAN * (g + 1)), piece, packed)
    return packed


def split(value):
    high = value.astype(jnp.bfloat16)
    return high, (value - high.astype(jnp.float32)).astype(jnp.bfloat16)


def dot(a, b):
    return jnp.dot(a, b, preferred_element_type=jnp.float32)


def transform(matrices, offset, high, low):
    table_high = matrices[offset : offset + 128]
    table_low = matrices[offset + 128 : offset + 256]
    return dot(table_high, high) + (dot(table_high, low) + dot(table_low, high))


def solve(packed, inc, spec, coef, shifts, matrices, select, out):
    points = jnp.concatenate(
        [inc[pl.ds(s, STEPS, stride=8), :] for s in range(DEPTH)], axis=1
    )
    spec[...] = transform(matrices, 0, *split(points))
    diffusion = [
        jnp.broadcast_to(time_step * packed[s : s + 1, :], (64, 128)) for s in range(DEPTH)
    ]
    weights = sweep_weights(SWEEPS)

    half = STEPS // 2
    real, imag = slice(0, half), slice(half, STEPS)
    one, two, b = [shifts[half * i : half * (i + 1)] for i in range(3)]
    for s in range(DEPTH):
        d = diffusion[s]
        p1, p2 = one + 4.0 * d, two + 4.0 * d
        inv = 1.0 / (p1 * p2 + b * b)
        q1, q2, qb = p2 * inv, p1 * inv, b * inv
        lanes = slice(128 * s, 128 * s + 128)
        sr, si = spec[real, lanes], spec[imag, lanes]
        cr, ci = q1 * sr + qb * si, q2 * si - qb * sr
        coef[0, real, lanes], coef[0, imag, lanes] = cr, ci
        coef[1, real, lanes], coef[1, imag, lanes] = q1 * d, q2 * d
        coef[2, real, lanes] = qb * d
        spec[real, lanes], spec[imag, lanes] = weights[0] * cr, weights[0] * ci

    row = lax.broadcasted_iota(jnp.int32, (256, 128), 0) % 128
    column = lax.broadcasted_iota(jnp.int32, (256, 128), 1)
    beside = jnp.where(jnp.abs(row - column) == 1, 1.0, 0.0).astype(jnp.bfloat16)

    for w in weights[1:]:
        fields = [spec[:, 128 * s : 128 * s + 128] for s in range(DEPTH)]
        parts = jnp.concatenate([jnp.concatenate(split(f), axis=1) for f in fields], axis=0)
        sides = dot(parts, beside)
        top, bottom = pltpu.roll(fields[-1], SPAN, 1), pltpu.roll(fields[0], 128 - SPAN, 1)
        for s in range(DEPTH):
            above = fields[s - 1] if s else top
            below = fields[s + 1] if s < DEPTH - 1 else bottom
            near = (above + below) + sides[128 * s : 128 * s + 128]
            nr, ni = near[:half], near[half:]
            lanes = slice(128 * s, 128 * s + 128)
            gb = coef[2, real, lanes]
            nr2 = coef[0, real, lanes] + coef[1, real, lanes] * nr + gb * ni
            ni2 = coef[0, imag, lanes] + coef[1, imag, lanes] * ni - gb * nr
            spec[real, lanes] = (1.0 - w) * fields[s][:half] + w * nr2
            spec[imag, lanes] = (1.0 - w) * fields[s][half:] + w * ni2

    high, low = split(spec[...])
    picked_high = dot(high, select[...]).astype(jnp.bfloat16)
    picked_low = dot(low, select[...]).astype(jnp.bfloat16)
    back = transform(matrices, 256, picked_high, picked_low)
    out[pl.ds(0, STEPS, stride=8), :] = back[:, :128]
    out[pl.ds(1, STEPS, stride=8), :] = back[:, 128:]


def main_kernel(
    src_in, it_in, ini_in, cnd_in, shifts_in, matrices_in, select_in,
    back_ref,
    it, src, prv, cnd, res, out, inc, spec, coef, out2, shifts, matrices, select,
    send_sem, recv_sem, local_sem, table_sem, a2a_sem, a2a2_sem, self_sem, ready,
):
    me = lax.axis_index("tm")
    slab = lax.axis_index("rows")
    y, z, core = me // 16, me // 2 % 8, me % 2
    after, before = (me + 1) % STEPS, (me + STEPS - 1) % STEPS
    down, up = (slab + 1) % 4, (slab + 3) % 4

    tables_in = [
        pltpu.make_async_copy(a, b, table_sem.at[i])
        for i, (a, b) in enumerate(
            [(shifts_in, shifts), (matrices_in, matrices), (select_in, select)]
        )
    ]
    inside = pl.ds(128, COLS)
    own = [
        pltpu.make_async_copy(it_in.at[0], it.at[pl.ds(8, ROWS)], local_sem.at[0]),
        pltpu.make_async_copy(src_in.at[0], src.at[pl.ds(8, ROWS)], local_sem.at[1]),
        pltpu.make_async_copy(cnd_in, cnd.at[pl.ds(8, ROWS), inside], local_sem.at[2]),
    ]
    barrier = pltpu.get_barrier_semaphore()

    def tell(sem, peer):
        pl.semaphore_signal(sem, inc=1, device_id=peer, device_id_type=MESH)

    greeted = [{"tm": after}, {"tm": before}, {"rows": down}, {"rows": up}]
    greeted += [{"tm": t, "rows": r} for t in (after, before) for r in (down, up)]
    for peer in greeted:
        tell(barrier, peer)
    low = z < 4
    for c in range(2):
        for collector, when in ((COLLECT_LOW + c, low), (COLLECT_ALL + c, True)):

            @pl.when(jnp.logical_and(me != collector, when))
            def _():
                tell(barrier, {"tm": collector})

    for copy in own + tables_in:
        copy.start()
    collects_low, collects_all = me // 2 == COLLECT_LOW // 2, me // 2 == COLLECT_ALL // 2
    heard = jnp.where(collects_low, STEPS // 2 - 1, 0) + jnp.where(collects_all, STEPS - 1, 0)
    pl.semaphore_wait(barrier, len(greeted) + heard)

    @pl.when(collects_low)
    def _():
        for dy in range(8):
            for plane in range(4):
                if 16 * dy + 2 * plane != COLLECT_LOW:
                    tell(ready.at[0], {"tm": 16 * dy + 2 * plane + core})
        pl.semaphore_signal(ready.at[0], inc=1)

    @pl.when(collects_all)
    def _():
        for dy, dz, dc in FAR_FIRST:
            if dc == 0:
                tell(ready.at[1], {"tm": (y + dy) % 8 * 16 + (z + dz) % 8 * 2 + core})
        pl.semaphore_signal(ready.at[1], inc=1)

    def remote(i, a, b, peer):
        return pltpu.make_async_remote_copy(
            a, b, send_sem.at[i], recv_sem.at[i], device_id=peer, device_id_type=MESH
        )

    def rows(ref, first, count):
        return ref.at[pl.ds(first, count)]

    it_own, src_own = it_in.at[0], src_in.at[0]

    def previous(value):
        return [
            remote(0, value, rows(prv, 8, ROWS), {"tm": after}),
            remote(1, rows(value, ROWS - HALO, HALO), rows(prv, TOP, HALO), {"tm": after, "rows": down}),
            remote(2, rows(value, 0, HALO), rows(prv, 8 + ROWS, HALO), {"tm": after, "rows": up}),
        ]

    @pl.when(me < STEPS - 1)
    def _():
        for copy in previous(it_own):
            copy.start()

    @pl.when(me == STEPS - 1)
    def _():
        for copy in previous(ini_in):
            copy.start()

    halos = [
        remote(3, rows(it_own, ROWS - HALO - 1, HALO + 1), rows(it, TOP - 1, HALO + 1), {"rows": down}),
        remote(4, rows(it_own, 0, HALO + 1), rows(it, 8 + ROWS, HALO + 1), {"rows": up}),
        remote(5, rows(src_own, ROWS - HALO, HALO), rows(src, TOP, HALO), {"rows": down}),
        remote(6, rows(src_own, 0, HALO), rows(src, 8 + ROWS, HALO), {"rows": up}),
        remote(7, rows(cnd_in, ROWS - HALO, HALO), cnd.at[pl.ds(TOP, HALO), inside], {"rows": down}),
        remote(8, rows(cnd_in, 0, HALO), cnd.at[pl.ds(8 + ROWS, HALO), inside], {"rows": up}),
    ]
    for copy in halos:
        copy.start()
    for copy in own:
        copy.wait()
    for copy in previous(ini_in) + halos:
        copy.wait()

    @pl.when(slab == 0)
    def _():
        for ref in (it, src, prv, cnd):
            ref[0:8, :] = jnp.zeros((8, ref.shape[1]), jnp.float32)

    @pl.when(slab == 3)
    def _():
        for ref in (it, src, prv, cnd):
            ref[8 + ROWS :, :] = jnp.zeros((8, ref.shape[1]), jnp.float32)

    residual_pack_send(me, y, z, core, it, src, prv, cnd, res, out, inc, a2a_sem, self_sem.at[0], ready)
    packed = own_conductivity(me, y, cnd)

    def wait_all(a, b, depth, sems, sem):
        share = (STEPS - 1) * depth
        pltpu.make_async_copy(rows(a, 0, depth), rows(b, 0, depth), sem).wait()
        pltpu.make_async_remote_copy(
            rows(a, 0, share), rows(b, 0, share), sems.at[0], sems.at[1],
            device_id={"tm": after}, device_id_type=MESH,
        ).wait()

    for copy in tables_in:
        copy.wait()
    wait_all(out, inc, DEPTH, a2a_sem, self_sem.at[0])
    solve(packed, inc, spec, coef, shifts, matrices, select, out2)

    mine = pl.ds(pl.multiple_of(8 * me, 8), 2)
    pltpu.make_async_copy(out2.at[mine], back_ref.at[mine], self_sem.at[1]).start()

    for dy, dz, dc in FAR_FIRST:
        peer = (y + dy) % 8 * 16 + (z + dz) % 8 * 2 + (core + dc) % 2
        pltpu.make_async_remote_copy(
            out2.at[pl.ds(pl.multiple_of(8 * peer, 8), 2)], back_ref.at[mine],
            a2a2_sem.at[0], a2a2_sem.at[1], device_id={"tm": peer}, device_id_type=MESH,
        ).start()

    wait_all(out2, back_ref, 2, a2a2_sem, self_sem.at[1])


def unpack_kernel(back, out, rows):
    block = lax.broadcasted_iota(jnp.int32, (8, 128), 1) // 8
    for h in range(2):
        v = [back[pl.ds(8 * tile + h, 8, stride=128), :] for tile in range(16)]
        for bit in (1, 2, 4, 8):
            there = (block & bit) != 0
            for tile in range(16):
                if not tile & bit:
                    p, q = v[tile], v[tile + bit]
                    v[tile] = jnp.where(there, pltpu.roll(q, 8 * bit, 1), p)
                    v[tile + bit] = jnp.where(there, q, pltpu.roll(p, 128 - 8 * bit, 1))
        for i in range(16):
            row = 16 * h + i
            rows[pl.ds(64 * (row // 8) + row % 8, 8, stride=8), :] = v[i]
    for i in range(ROWS // 8):
        for group in range(8):
            out[0, 8 * i : 8 * i + 8, 128 * group : 128 * group + 128] = rows[
                64 * i + 8 * group : 64 * i + 8 * group + 8
            ]


def shards(source_term, iterate, initial, conductivity):
    shifts, matrices, select = tables()
    f32 = jnp.float32
    dma = pltpu.SemaphoreType.DMA
    back = pl.pallas_call(
        main_kernel,
        out_shape=jax.ShapeDtypeStruct((1024, 128), f32),
        in_specs=[pl.BlockSpec(memory_space=pl.ANY)] * 7,
        out_specs=pl.BlockSpec(memory_space=pl.ANY),
        scratch_shapes=[
            pltpu.VMEM((FRAME, COLS), f32),
            pltpu.VMEM((FRAME, COLS), f32),
            pltpu.VMEM((FRAME, COLS), f32),
            pltpu.VMEM((FRAME, COLS + 256), f32),
            pltpu.VMEM((FRAME, COLS + 256), f32),
            pltpu.VMEM((1024, 128), f32),
            pltpu.VMEM((1024, 128), f32),
            pltpu.VMEM((128, DEPTH * 128), f32),
            pltpu.VMEM((3, 128, DEPTH * 128), f32),
            pltpu.VMEM((1024, 128), f32),
            pltpu.VMEM(shifts.shape, f32),
            pltpu.VMEM(matrices.shape, jnp.bfloat16),
            pltpu.VMEM(select.shape, jnp.bfloat16),
            dma((9,)), dma((9,)), dma((3,)), dma((3,)), dma((2,)), dma((2,)), dma((2,)),
            pltpu.SemaphoreType.REGULAR((2,)),
        ],
        compiler_params=pltpu.CompilerParams(collective_id=0, has_side_effects=True),
        name="main",
    )(source_term, iterate, initial, conductivity, shifts, matrices, select)
    return pl.pallas_call(
        unpack_kernel,
        out_shape=jax.ShapeDtypeStruct((1, ROWS, COLS), f32),
        in_specs=[pl.BlockSpec(memory_space=pltpu.VMEM)],
        out_specs=pl.BlockSpec(memory_space=pltpu.VMEM),
        scratch_shapes=[pltpu.VMEM((8 * ROWS, 128), f32)],
        name="unpack",
    )(back)


def solution(mesh):
    in_specs = (P("tm", "rows", None), P("tm", "rows", None), P("rows", None), P("rows", None))
    out_specs = P("tm", "rows", None)
    return jax.shard_map(shards, mesh=mesh, in_specs=in_specs, out_specs=out_specs, check_vma=False)
```

```python
import functools
import math

import jax
import jax.numpy as jnp
import numpy as np
from jax import lax
from jax.experimental import pallas as pl
from jax.experimental.pallas import tpu as pltpu
from jax.sharding import PartitionSpec as P

MESH = pl.DeviceIdType.MESH

SWEEPS = 6
time_step = 0.5
wrap_factor = 0.25
chebyshev_spread = 0.7

STEPS = 128
COLS = 1024
ROWS = 32
TILE = 8
HALO = SWEEPS - 1
COLLECT_LOW = 16 * 5 + 2 * 2
COLLECT_ALL = 16 * 5 + 2 * 5
FAR_ROWS = (4, 3, 5, 2, 6, 1, 7, 0)
FAR_FIRST = sorted(
    [(dy, dz, dc) for dy in range(8) for dz in range(8) for dc in range(2) if dy or dz or dc],
    key=lambda d: -min(d[0], 8 - d[0]) - min(d[1], 8 - d[1]),
)
SPAN = TILE + 2 * HALO
GROUPS = 7
DEPTH = 6
TOP = 8 - HALO
FRAME = ROWS + 16


def sweep_weights(count):
    return [
        1.0 / (1.0 + chebyshev_spread * math.cos(math.pi * (2 * sweep + 1) / (2 * count)))
        for sweep in range(count)
    ]


def tables():
    half = STEPS // 2
    k = np.arange(half)
    n = np.arange(STEPS)
    angle = 2.0 * np.pi * (k[:, None] * n[None, :] % STEPS) / STEPS
    weight = wrap_factor ** (n / STEPS)
    cosine, sine = np.cos(angle), np.sin(angle)
    alternating = np.where(n % 2 == 0, 1.0, -1.0)
    forward = np.concatenate([cosine, -sine]) * weight
    forward[half] = alternating * weight
    multiplicity = np.where(k == 0, 1.0, 2.0)[:, None]
    inverse = np.concatenate([cosine * multiplicity, -2.0 * sine])
    inverse[half] = alternating
    inverse = (inverse / (STEPS * weight)).T
    beta = wrap_factor ** (1.0 / STEPS)
    theta = 2.0 * np.pi * k / STEPS
    shift_one = 1.0 - beta * np.cos(theta)
    shift_two = shift_one.copy()
    shift_two[0] = 1.0 + beta
    coupling = beta * np.sin(theta)
    coupling[0] = 0.0
    wide = [np.repeat(v[:, None], 128, axis=1) for v in (shift_one, shift_two, coupling)]
    shifts = np.concatenate(wide).astype(np.float32)

    def parts(matrix):
        whole = matrix.astype(np.float32)
        high = whole.astype(jnp.bfloat16)
        low = (whole - high.astype(np.float32)).astype(jnp.bfloat16)
        return [high, low]

    select = np.zeros((DEPTH * 128, 256), np.float32)
    for row in range(ROWS):
        g, s = divmod(row + HALO, DEPTH)
        for c in range(TILE):
            select[128 * s + SPAN * g + HALO + c, 128 * (row // 16) + 8 * (row % 16) + c] = 1.0
    matrices = np.concatenate(parts(forward) + parts(inverse))
    return shifts, matrices, select.astype(jnp.bfloat16)


def residual_pack_send(me, y, z, core, it, src, prv, cnd, res, out, inc, sems, local_sem, ready):
    lane = lax.broadcasted_iota(jnp.int32, (8, 128), 1)
    column = lax.broadcasted_iota(jnp.int32, (FRAME, COLS), 1)
    field = it[...]
    left = jnp.where(column == 0, 0.0, pltpu.roll(field, 1, 1))
    right = jnp.where(column == COLS - 1, 0.0, pltpu.roll(field, COLS - 1, 1))
    lap = 4.0 * field - pltpu.roll(field, 1, 0) - pltpu.roll(field, FRAME - 1, 0) - left - right
    operated = cnd[:, 128 : 128 + COLS] * lap
    res[:, 128 : 128 + COLS] = src[...] - (field + time_step * operated - prv[...])
    zero = jnp.zeros((FRAME, 128), jnp.float32)
    for ref in (res, cnd):
        ref[:, :128] = zero
        ref[:, 128 + COLS :] = zero

    def send(peer):
        pltpu.make_async_remote_copy(
            out.at[pl.ds(pl.multiple_of(8 * peer, 8), DEPTH)],
            inc.at[pl.ds(pl.multiple_of(8 * me, 8), DEPTH)],
            sems.at[0], sems.at[1], device_id={"tm": peer}, device_id_type=MESH,
        ).start()

    pl.semaphore_wait(ready.at[z // 4], 1)
    low = z < 4

    @pl.loop(0, 8)
    def _(i):
        half = (i + 1) // 2
        t = (y + 4 + jnp.where(i % 2 == 0, half, -half) + 8) % 8
        plain, first, last = [], [], []
        for g in range(GROUPS):
            rows = pl.ds(TOP + DEPTH * g, 8)
            before, strip, after = [
                res[rows, pl.ds(pl.multiple_of(128 * t + 128 * d, 128), 128)] for d in range(3)
            ]
            amount = SPAN * g + HALO
            plain.append(pltpu.roll(strip, amount, 1))
            first.append(pltpu.roll(jnp.where(lane >= 64, before, strip), amount, 1))
            last.append(pltpu.roll(jnp.where(lane < 64, after, strip), amount, 1))
        for jj in range(16):
            strips = first if jj == 0 else last if jj == 15 else plain
            place = (lane + (128 - TILE * jj)) % 128
            message = strips[0]
            for g in range(1, GROUPS):
                message = jnp.where(place >= SPAN * g, strips[g], message)
            out[pl.ds(pl.multiple_of(128 * t + 8 * jj, 8), 8)] = pltpu.roll(
                message, (128 - TILE * jj) % 128, 1
            )
        for turn in range(1, 4):
            for c in range(2):
                send(16 * t + 2 * (z // 4 * 4 + (z + turn) % 4) + c)
        send(16 * t + 2 * z + 1 - core)

        @pl.when(t != y)
        def _():
            send(16 * t + 2 * z + core)

        @pl.when(jnp.logical_not(low))
        def _():
            for plane in range(4):
                for c in range(2):
                    send(16 * t + 2 * plane + c)

    mine = pl.ds(pl.multiple_of(8 * me, 8), DEPTH)
    pltpu.make_async_copy(out.at[mine], inc.at[mine], local_sem).start()

    @pl.when(low)
    def _():
        pl.semaphore_wait(ready.at[1], 1)

        @pl.loop(0, 8)
        def _(i):
            half = (i + 1) // 2
            t = (y + 4 + jnp.where(i % 2 == 0, half, -half) + 8) % 8
            for plane in range(4, 8):
                for c in range(2):
                    send(16 * t + 2 * plane + c)


def own_conductivity(me, y, cnd):
    lane = lax.broadcasted_iota(jnp.int32, (8, 128), 1)
    jj = me % 16
    packed = jnp.zeros((8, 128), jnp.float32)
    for g in range(GROUPS):
        rows = pl.ds(TOP + DEPTH * g, 8)
        before, strip, after = [
            cnd[rows, pl.ds(pl.multiple_of(128 * y + 128 * d, 128), 128)] for d in range(3)
        ]
        strip = jnp.where((jj == 0) & (lane >= 64), before, strip)
        strip = jnp.where((jj == 15) & (lane < 64), after, strip)
        amount = (SPAN * g - TILE * jj + HALO + 128) % 128
        piece = pltpu.roll(strip, amount, 1)
        packed = jnp.where((lane >= SPAN * g) & (lane < SPAN * (g + 1)), piece, packed)
    return packed


def split(value):
    high = value.astype(jnp.bfloat16)
    return high, (value - high.astype(jnp.float32)).astype(jnp.bfloat16)


def dot(a, b):
    return jnp.dot(a, b, preferred_element_type=jnp.float32)


def transform(matrices, offset, high, low):
    table_high = matrices[offset : offset + 128]
    table_low = matrices[offset + 128 : offset + 256]
    return dot(table_high, high) + (dot(table_high, low) + dot(table_low, high))


def prepare(packed, coef, shifts):
    half = STEPS // 2
    real, imag = slice(0, half), slice(half, STEPS)
    one, two, b = [shifts[half * i : half * (i + 1)] for i in range(3)]
    for s in range(DEPTH):
        d = jnp.broadcast_to(time_step * packed[s : s + 1, :], (half, 128))
        p1, p2 = one + 4.0 * d, two + 4.0 * d
        inv = 1.0 / (p1 * p2 + b * b)
        q1, q2, qb = p2 * inv, p1 * inv, b * inv
        lanes = slice(128 * s, 128 * s + 128)
        coef[0, real, lanes], coef[0, imag, lanes] = q1, q2
        coef[1, real, lanes], coef[1, imag, lanes] = q1 * d, q2 * d
        coef[2, real, lanes], coef[2, imag, lanes] = qb * d, qb


def solve(inc, spec, coef, matrices, select, out):
    points = jnp.concatenate(
        [inc[pl.ds(s, STEPS, stride=8), :] for s in range(DEPTH)], axis=1
    )
    spec[...] = transform(matrices, 0, *split(points))
    weights = sweep_weights(SWEEPS)

    half = STEPS // 2
    real, imag = slice(0, half), slice(half, STEPS)
    for s in range(DEPTH):
        lanes = slice(128 * s, 128 * s + 128)
        sr, si = spec[real, lanes], spec[imag, lanes]
        qb = coef[2, imag, lanes]
        cr = coef[0, real, lanes] * sr + qb * si
        ci = coef[0, imag, lanes] * si - qb * sr
        coef[0, real, lanes], coef[0, imag, lanes] = cr, ci
        spec[real, lanes], spec[imag, lanes] = weights[0] * cr, weights[0] * ci

    row = lax.broadcasted_iota(jnp.int32, (256, 128), 0) % 128
    column = lax.broadcasted_iota(jnp.int32, (256, 128), 1)
    beside = jnp.where(jnp.abs(row - column) == 1, 1.0, 0.0).astype(jnp.bfloat16)

    for w in weights[1:]:
        fields = [spec[:, 128 * s : 128 * s + 128] for s in range(DEPTH)]
        parts = jnp.concatenate([jnp.concatenate(split(f), axis=1) for f in fields], axis=0)
        sides = dot(parts, beside)
        top, bottom = pltpu.roll(fields[-1], SPAN, 1), pltpu.roll(fields[0], 128 - SPAN, 1)
        for s in range(DEPTH):
            above = fields[s - 1] if s else top
            below = fields[s + 1] if s < DEPTH - 1 else bottom
            near = (above + below) + sides[128 * s : 128 * s + 128]
            nr, ni = near[:half], near[half:]
            lanes = slice(128 * s, 128 * s + 128)
            gb = coef[2, real, lanes]
            nr2 = coef[0, real, lanes] + coef[1, real, lanes] * nr + gb * ni
            ni2 = coef[0, imag, lanes] + coef[1, imag, lanes] * ni - gb * nr
            spec[real, lanes] = (1.0 - w) * fields[s][:half] + w * nr2
            spec[imag, lanes] = (1.0 - w) * fields[s][half:] + w * ni2

    high, low = split(spec[...])
    picked_high = dot(high, select[...]).astype(jnp.bfloat16)
    picked_low = dot(low, select[...]).astype(jnp.bfloat16)
    back = transform(matrices, 256, picked_high, picked_low)
    out[pl.ds(0, STEPS, stride=8), :] = back[:, :128]
    out[pl.ds(1, STEPS, stride=8), :] = back[:, 128:]


def main_kernel(
    src_in, it_in, ini_in, cnd_in, shifts_in, matrices_in, select_in,
    back_ref,
    it, src, prv, cnd, res, out, inc, spec, coef, out2, shifts, matrices, select,
    send_sem, recv_sem, local_sem, table_sem, a2a_sem, a2a2_sem, self_sem, ready,
):
    me = lax.axis_index("tm")
    slab = lax.axis_index("rows")
    y, z, core = me // 16, me // 2 % 8, me % 2
    after, before = (me + 1) % STEPS, (me + STEPS - 1) % STEPS
    down, up = (slab + 1) % 4, (slab + 3) % 4

    tables_in = [
        pltpu.make_async_copy(a, b, table_sem.at[i])
        for i, (a, b) in enumerate(
            [(shifts_in, shifts), (matrices_in, matrices), (select_in, select)]
        )
    ]
    inside = pl.ds(128, COLS)
    own = [
        pltpu.make_async_copy(it_in.at[0], it.at[pl.ds(8, ROWS)], local_sem.at[0]),
        pltpu.make_async_copy(src_in.at[0], src.at[pl.ds(8, ROWS)], local_sem.at[1]),
        pltpu.make_async_copy(cnd_in, cnd.at[pl.ds(8, ROWS), inside], local_sem.at[2]),
    ]
    barrier = pltpu.get_barrier_semaphore()

    def tell(sem, peer):
        pl.semaphore_signal(sem, inc=1, device_id=peer, device_id_type=MESH)

    greeted = [{"tm": after}, {"tm": before}, {"rows": down}, {"rows": up}]
    greeted += [{"tm": t, "rows": r} for t in (after, before) for r in (down, up)]
    for peer in greeted:
        tell(barrier, peer)
    low = z < 4
    for c in range(2):
        for collector, when in ((COLLECT_LOW + c, low), (COLLECT_ALL + c, True)):

            @pl.when(jnp.logical_and(me != collector, when))
            def _():
                tell(barrier, {"tm": collector})

    for copy in own + tables_in:
        copy.start()
    collects_low, collects_all = me // 2 == COLLECT_LOW // 2, me // 2 == COLLECT_ALL // 2
    heard = jnp.where(collects_low, STEPS // 2 - 1, 0) + jnp.where(collects_all, STEPS - 1, 0)
    pl.semaphore_wait(barrier, len(greeted) + heard)

    def remote(i, a, b, peer):
        return pltpu.make_async_remote_copy(
            a, b, send_sem.at[i], recv_sem.at[i], device_id=peer, device_id_type=MESH
        )

    def rows(ref, first, count):
        return ref.at[pl.ds(first, count)]

    it_own, src_own = it_in.at[0], src_in.at[0]

    def previous(value):
        return [
            remote(0, value, rows(prv, 8, ROWS), {"tm": after}),
            remote(1, rows(value, ROWS - HALO, HALO), rows(prv, TOP, HALO), {"tm": after, "rows": down}),
            remote(2, rows(value, 0, HALO), rows(prv, 8 + ROWS, HALO), {"tm": after, "rows": up}),
        ]

    @pl.when(me < STEPS - 1)
    def _():
        for copy in previous(it_own):
            copy.start()

    @pl.when(me == STEPS - 1)
    def _():
        for copy in previous(ini_in):
            copy.start()

    halos = [
        remote(3, rows(it_own, ROWS - HALO - 1, HALO + 1), rows(it, TOP - 1, HALO + 1), {"rows": down}),
        remote(4, rows(it_own, 0, HALO + 1), rows(it, 8 + ROWS, HALO + 1), {"rows": up}),
        remote(5, rows(src_own, ROWS - HALO, HALO), rows(src, TOP, HALO), {"rows": down}),
        remote(6, rows(src_own, 0, HALO), rows(src, 8 + ROWS, HALO), {"rows": up}),
        remote(7, rows(cnd_in, ROWS - HALO, HALO), cnd.at[pl.ds(TOP, HALO), inside], {"rows": down}),
        remote(8, rows(cnd_in, 0, HALO), cnd.at[pl.ds(8 + ROWS, HALO), inside], {"rows": up}),
    ]
    for copy in halos:
        copy.start()

    @pl.when(collects_low)
    def _():
        for dy in range(8):
            for plane in range(4):
                if 16 * dy + 2 * plane != COLLECT_LOW:
                    tell(ready.at[0], {"tm": 16 * dy + 2 * plane + core})
        pl.semaphore_signal(ready.at[0], inc=1)

    @pl.when(collects_all)
    def _():
        for dy, dz, dc in FAR_FIRST:
            if dc == 0:
                tell(ready.at[1], {"tm": (y + dy) % 8 * 16 + (z + dz) % 8 * 2 + core})
        pl.semaphore_signal(ready.at[1], inc=1)

    for copy in own:
        copy.wait()
    for copy in previous(ini_in) + halos:
        copy.wait()

    @pl.when(slab == 0)
    def _():
        for ref in (it, src, prv, cnd):
            ref[0:8, :] = jnp.zeros((8, ref.shape[1]), jnp.float32)

    @pl.when(slab == 3)
    def _():
        for ref in (it, src, prv, cnd):
            ref[8 + ROWS :, :] = jnp.zeros((8, ref.shape[1]), jnp.float32)

    residual_pack_send(me, y, z, core, it, src, prv, cnd, res, out, inc, a2a_sem, self_sem.at[0], ready)
    packed = own_conductivity(me, y, cnd)

    def wait_all(a, b, depth, sems, sem):
        share = (STEPS - 1) * depth
        pltpu.make_async_copy(rows(a, 0, depth), rows(b, 0, depth), sem).wait()
        pltpu.make_async_remote_copy(
            rows(a, 0, share), rows(b, 0, share), sems.at[0], sems.at[1],
            device_id={"tm": after}, device_id_type=MESH,
        ).wait()

    for copy in tables_in:
        copy.wait()
    prepare(packed, coef, shifts)
    wait_all(out, inc, DEPTH, a2a_sem, self_sem.at[0])
    solve(inc, spec, coef, matrices, select, out2)

    mine = pl.ds(pl.multiple_of(8 * me, 8), 2)
    pltpu.make_async_copy(out2.at[mine], back_ref.at[mine], self_sem.at[1]).start()

    for dy, dz, dc in FAR_FIRST:
        peer = (y + dy) % 8 * 16 + (z + dz) % 8 * 2 + (core + dc) % 2
        pltpu.make_async_remote_copy(
            out2.at[pl.ds(pl.multiple_of(8 * peer, 8), 2)], back_ref.at[mine],
            a2a2_sem.at[0], a2a2_sem.at[1], device_id={"tm": peer}, device_id_type=MESH,
        ).start()

    wait_all(out2, back_ref, 2, a2a2_sem, self_sem.at[1])


def unpack_kernel(back, out, rows):
    block = lax.broadcasted_iota(jnp.int32, (8, 128), 1) // 8
    for h in range(2):
        v = [back[pl.ds(8 * tile + h, 8, stride=128), :] for tile in range(16)]
        for bit in (1, 2, 4, 8):
            there = (block & bit) != 0
            for tile in range(16):
                if not tile & bit:
                    p, q = v[tile], v[tile + bit]
                    v[tile] = jnp.where(there, pltpu.roll(q, 8 * bit, 1), p)
                    v[tile + bit] = jnp.where(there, q, pltpu.roll(p, 128 - 8 * bit, 1))
        for i in range(16):
            row = 16 * h + i
            rows[pl.ds(64 * (row // 8) + row % 8, 8, stride=8), :] = v[i]
    for i in range(ROWS // 8):
        for group in range(8):
            out[0, 8 * i : 8 * i + 8, 128 * group : 128 * group + 128] = rows[
                64 * i + 8 * group : 64 * i + 8 * group + 8
            ]


def shards(source_term, iterate, initial, conductivity):
    shifts, matrices, select = tables()
    f32 = jnp.float32
    dma = pltpu.SemaphoreType.DMA
    back = pl.pallas_call(
        main_kernel,
        out_shape=jax.ShapeDtypeStruct((1024, 128), f32),
        in_specs=[pl.BlockSpec(memory_space=pl.ANY)] * 7,
        out_specs=pl.BlockSpec(memory_space=pl.ANY),
        scratch_shapes=[
            pltpu.VMEM((FRAME, COLS), f32),
            pltpu.VMEM((FRAME, COLS), f32),
            pltpu.VMEM((FRAME, COLS), f32),
            pltpu.VMEM((FRAME, COLS + 256), f32),
            pltpu.VMEM((FRAME, COLS + 256), f32),
            pltpu.VMEM((1024, 128), f32),
            pltpu.VMEM((1024, 128), f32),
            pltpu.VMEM((128, DEPTH * 128), f32),
            pltpu.VMEM((3, 128, DEPTH * 128), f32),
            pltpu.VMEM((1024, 128), f32),
            pltpu.VMEM(shifts.shape, f32),
            pltpu.VMEM(matrices.shape, jnp.bfloat16),
            pltpu.VMEM(select.shape, jnp.bfloat16),
            dma((9,)), dma((9,)), dma((3,)), dma((3,)), dma((2,)), dma((2,)), dma((2,)),
            pltpu.SemaphoreType.REGULAR((2,)),
        ],
        compiler_params=pltpu.CompilerParams(collective_id=0, has_side_effects=True),
        name="main",
    )(source_term, iterate, initial, conductivity, shifts, matrices, select)
    return pl.pallas_call(
        unpack_kernel,
        out_shape=jax.ShapeDtypeStruct((1, ROWS, COLS), f32),
        in_specs=[pl.BlockSpec(memory_space=pltpu.VMEM)],
        out_specs=pl.BlockSpec(memory_space=pltpu.VMEM),
        scratch_shapes=[pltpu.VMEM((8 * ROWS, 128), f32)],
        name="unpack",
    )(back)


def solution(mesh):
    in_specs = (P("tm", "rows", None), P("tm", "rows", None), P("rows", None), P("rows", None))
    out_specs = P("tm", "rows", None)
    return jax.shard_map(shards, mesh=mesh, in_specs=in_specs, out_specs=out_specs, check_vma=False)
```

```python
import functools
import math

import jax
import jax.numpy as jnp
import numpy as np
from jax import lax
from jax.experimental import pallas as pl
from jax.experimental.pallas import tpu as pltpu
from jax.sharding import PartitionSpec as P

MESH = pl.DeviceIdType.MESH

SWEEPS = 6
time_step = 0.5
wrap_factor = 0.25
chebyshev_spread = 0.7

STEPS = 128
COLS = 1024
ROWS = 32
TILE = 8
HALO = SWEEPS - 1
COLLECT_LOW = 16 * 5 + 2 * 2
COLLECT_ALL = 16 * 5 + 2 * 5
FAR_ROWS = (4, 3, 5, 2, 6, 1, 7, 0)
FAR_FIRST = sorted(
    [(dy, dz, dc) for dy in range(8) for dz in range(8) for dc in range(2) if dy or dz or dc],
    key=lambda d: -min(d[0], 8 - d[0]) - min(d[1], 8 - d[1]),
)
SPAN = TILE + 2 * HALO
GROUPS = 7
DEPTH = 6
TOP = 8 - HALO
FRAME = ROWS + 16


def sweep_weights(count):
    return [
        1.0 / (1.0 + chebyshev_spread * math.cos(math.pi * (2 * sweep + 1) / (2 * count)))
        for sweep in range(count)
    ]


def tables():
    half = STEPS // 2
    k = np.arange(half)
    n = np.arange(STEPS)
    angle = 2.0 * np.pi * (k[:, None] * n[None, :] % STEPS) / STEPS
    weight = wrap_factor ** (n / STEPS)
    cosine, sine = np.cos(angle), np.sin(angle)
    alternating = np.where(n % 2 == 0, 1.0, -1.0)
    forward = np.concatenate([cosine, -sine]) * weight
    forward[half] = alternating * weight
    multiplicity = np.where(k == 0, 1.0, 2.0)[:, None]
    inverse = np.concatenate([cosine * multiplicity, -2.0 * sine])
    inverse[half] = alternating
    inverse = (inverse / (STEPS * weight)).T
    beta = wrap_factor ** (1.0 / STEPS)
    theta = 2.0 * np.pi * k / STEPS
    shift_one = 1.0 - beta * np.cos(theta)
    shift_two = shift_one.copy()
    shift_two[0] = 1.0 + beta
    coupling = beta * np.sin(theta)
    coupling[0] = 0.0
    wide = [np.repeat(v[:, None], 128, axis=1) for v in (shift_one, shift_two, coupling)]
    shifts = np.concatenate(wide).astype(np.float32)

    def parts(matrix):
        whole = matrix.astype(np.float32)
        high = whole.astype(jnp.bfloat16)
        low = (whole - high.astype(np.float32)).astype(jnp.bfloat16)
        return [high, low]

    select = np.zeros((DEPTH * 128, 256), np.float32)
    for row in range(ROWS):
        g, s = divmod(row + HALO, DEPTH)
        for c in range(TILE):
            select[128 * s + SPAN * g + HALO + c, 128 * (row // 16) + 8 * (row % 16) + c] = 1.0
    matrices = np.concatenate(parts(forward) + parts(inverse))
    return shifts, matrices, select.astype(jnp.bfloat16)


def residual_pack_send(me, y, z, core, it, src, prv, cnd, res, out, inc, sems, local_sem, ready):
    lane = lax.broadcasted_iota(jnp.int32, (8, 128), 1)
    column = lax.broadcasted_iota(jnp.int32, (FRAME, COLS), 1)
    field = it[...]
    left = jnp.where(column == 0, 0.0, pltpu.roll(field, 1, 1))
    right = jnp.where(column == COLS - 1, 0.0, pltpu.roll(field, COLS - 1, 1))
    lap = 4.0 * field - pltpu.roll(field, 1, 0) - pltpu.roll(field, FRAME - 1, 0) - left - right
    operated = cnd[:, 128 : 128 + COLS] * lap
    res[:, 128 : 128 + COLS] = src[...] - (field + time_step * operated - prv[...])
    zero = jnp.zeros((FRAME, 128), jnp.float32)
    for ref in (res, cnd):
        ref[:, :128] = zero
        ref[:, 128 + COLS :] = zero

    def send(peer):
        pltpu.make_async_remote_copy(
            out.at[pl.ds(pl.multiple_of(8 * peer, 8), DEPTH)],
            inc.at[pl.ds(pl.multiple_of(8 * me, 8), DEPTH)],
            sems.at[0], sems.at[1], device_id={"tm": peer}, device_id_type=MESH,
        ).start()

    pl.semaphore_wait(ready.at[z // 4], 1)
    low = z < 4

    @pl.loop(0, 8)
    def _(i):
        half = (i + 1) // 2
        t = (y + 4 + jnp.where(i % 2 == 0, half, -half) + 8) % 8
        plain, first, last = [], [], []
        for g in range(GROUPS):
            rows = pl.ds(TOP + DEPTH * g, 8)
            before, strip, after = [
                res[rows, pl.ds(pl.multiple_of(128 * t + 128 * d, 128), 128)] for d in range(3)
            ]
            amount = SPAN * g + HALO
            plain.append(pltpu.roll(strip, amount, 1))
            first.append(pltpu.roll(jnp.where(lane >= 64, before, strip), amount, 1))
            last.append(pltpu.roll(jnp.where(lane < 64, after, strip), amount, 1))
        for jj in range(16):
            strips = first if jj == 0 else last if jj == 15 else plain
            place = (lane + (128 - TILE * jj)) % 128
            message = strips[0]
            for g in range(1, GROUPS):
                message = jnp.where(place >= SPAN * g, strips[g], message)
            out[pl.ds(pl.multiple_of(128 * t + 8 * jj, 8), 8)] = pltpu.roll(
                message, (128 - TILE * jj) % 128, 1
            )
        for turn in range(1, 4):
            for c in range(2):
                send(16 * t + 2 * (z // 4 * 4 + (z + turn) % 4) + c)
        send(16 * t + 2 * z + 1 - core)

        @pl.when(t != y)
        def _():
            send(16 * t + 2 * z + core)

        @pl.when(jnp.logical_not(low))
        def _():
            for plane in range(4):
                for c in range(2):
                    send(16 * t + 2 * plane + c)

    mine = pl.ds(pl.multiple_of(8 * me, 8), DEPTH)
    pltpu.make_async_copy(out.at[mine], inc.at[mine], local_sem).start()

    @pl.when(low)
    def _():
        pl.semaphore_wait(ready.at[1], 1)

        @pl.loop(0, 8)
        def _(i):
            t = (y + i) % 4 + jnp.where(i < 4, 4, 0)
            for plane in range(4, 8):
                for c in range(2):
                    send(16 * t + 2 * plane + c)


def own_conductivity(me, y, cnd):
    lane = lax.broadcasted_iota(jnp.int32, (8, 128), 1)
    jj = me % 16
    packed = jnp.zeros((8, 128), jnp.float32)
    for g in range(GROUPS):
        rows = pl.ds(TOP + DEPTH * g, 8)
        before, strip, after = [
            cnd[rows, pl.ds(pl.multiple_of(128 * y + 128 * d, 128), 128)] for d in range(3)
        ]
        strip = jnp.where((jj == 0) & (lane >= 64), before, strip)
        strip = jnp.where((jj == 15) & (lane < 64), after, strip)
        amount = (SPAN * g - TILE * jj + HALO + 128) % 128
        piece = pltpu.roll(strip, amount, 1)
        packed = jnp.where((lane >= SPAN * g) & (lane < SPAN * (g + 1)), piece, packed)
    return packed


def split(value):
    high = value.astype(jnp.bfloat16)
    return high, (value - high.astype(jnp.float32)).astype(jnp.bfloat16)


def dot(a, b):
    return jnp.dot(a, b, preferred_element_type=jnp.float32)


def transform(matrices, offset, high, low):
    table_high = matrices[offset : offset + 128]
    table_low = matrices[offset + 128 : offset + 256]
    return dot(table_high, high) + (dot(table_high, low) + dot(table_low, high))


def prepare(packed, coef, shifts):
    half = STEPS // 2
    real, imag = slice(0, half), slice(half, STEPS)
    one, two, b = [shifts[half * i : half * (i + 1)] for i in range(3)]
    for s in range(DEPTH):
        d = jnp.broadcast_to(time_step * packed[s : s + 1, :], (half, 128))
        p1, p2 = one + 4.0 * d, two + 4.0 * d
        inv = 1.0 / (p1 * p2 + b * b)
        q1, q2, qb = p2 * inv, p1 * inv, b * inv
        lanes = slice(128 * s, 128 * s + 128)
        coef[0, real, lanes], coef[0, imag, lanes] = q1, q2
        coef[1, real, lanes], coef[1, imag, lanes] = q1 * d, q2 * d
        coef[2, real, lanes], coef[2, imag, lanes] = qb * d, qb


def solve(inc, spec, coef, matrices, select, out):
    points = jnp.concatenate(
        [inc[pl.ds(s, STEPS, stride=8), :] for s in range(DEPTH)], axis=1
    )
    spec[...] = transform(matrices, 0, *split(points))
    weights = sweep_weights(SWEEPS)

    half = STEPS // 2
    real, imag = slice(0, half), slice(half, STEPS)
    for s in range(DEPTH):
        lanes = slice(128 * s, 128 * s + 128)
        sr, si = spec[real, lanes], spec[imag, lanes]
        qb = coef[2, imag, lanes]
        cr = coef[0, real, lanes] * sr + qb * si
        ci = coef[0, imag, lanes] * si - qb * sr
        coef[0, real, lanes], coef[0, imag, lanes] = cr, ci
        spec[real, lanes], spec[imag, lanes] = weights[0] * cr, weights[0] * ci

    row = lax.broadcasted_iota(jnp.int32, (256, 128), 0) % 128
    column = lax.broadcasted_iota(jnp.int32, (256, 128), 1)
    beside = jnp.where(jnp.abs(row - column) == 1, 1.0, 0.0).astype(jnp.bfloat16)

    for w in weights[1:]:
        fields = [spec[:, 128 * s : 128 * s + 128] for s in range(DEPTH)]
        parts = jnp.concatenate([jnp.concatenate(split(f), axis=1) for f in fields], axis=0)
        sides = dot(parts, beside)
        top, bottom = pltpu.roll(fields[-1], SPAN, 1), pltpu.roll(fields[0], 128 - SPAN, 1)
        for s in range(DEPTH):
            above = fields[s - 1] if s else top
            below = fields[s + 1] if s < DEPTH - 1 else bottom
            near = (above + below) + sides[128 * s : 128 * s + 128]
            nr, ni = near[:half], near[half:]
            lanes = slice(128 * s, 128 * s + 128)
            gb = coef[2, real, lanes]
            nr2 = coef[0, real, lanes] + coef[1, real, lanes] * nr + gb * ni
            ni2 = coef[0, imag, lanes] + coef[1, imag, lanes] * ni - gb * nr
            spec[real, lanes] = (1.0 - w) * fields[s][:half] + w * nr2
            spec[imag, lanes] = (1.0 - w) * fields[s][half:] + w * ni2

    high, low = split(spec[...])
    picked_high = dot(high, select[...]).astype(jnp.bfloat16)
    picked_low = dot(low, select[...]).astype(jnp.bfloat16)
    back = transform(matrices, 256, picked_high, picked_low)
    out[pl.ds(0, STEPS, stride=8), :] = back[:, :128]
    out[pl.ds(1, STEPS, stride=8), :] = back[:, 128:]


def main_kernel(
    src_in, it_in, ini_in, cnd_in, shifts_in, matrices_in, select_in,
    back_ref,
    it, src, prv, cnd, res, out, inc, spec, coef, out2, shifts, matrices, select,
    send_sem, recv_sem, local_sem, table_sem, a2a_sem, a2a2_sem, self_sem, ready,
):
    me = lax.axis_index("tm")
    slab = lax.axis_index("rows")
    y, z, core = me // 16, me // 2 % 8, me % 2
    after, before = (me + 1) % STEPS, (me + STEPS - 1) % STEPS
    down, up = (slab + 1) % 4, (slab + 3) % 4

    tables_in = [
        pltpu.make_async_copy(a, b, table_sem.at[i])
        for i, (a, b) in enumerate(
            [(shifts_in, shifts), (matrices_in, matrices), (select_in, select)]
        )
    ]
    inside = pl.ds(128, COLS)
    own = [
        pltpu.make_async_copy(it_in.at[0], it.at[pl.ds(8, ROWS)], local_sem.at[0]),
        pltpu.make_async_copy(src_in.at[0], src.at[pl.ds(8, ROWS)], local_sem.at[1]),
        pltpu.make_async_copy(cnd_in, cnd.at[pl.ds(8, ROWS), inside], local_sem.at[2]),
    ]
    barrier = pltpu.get_barrier_semaphore()

    def tell(sem, peer):
        pl.semaphore_signal(sem, inc=1, device_id=peer, device_id_type=MESH)

    greeted = [{"tm": after}, {"tm": before}, {"rows": down}, {"rows": up}]
    greeted += [{"tm": t, "rows": r} for t in (after, before) for r in (down, up)]
    for peer in greeted:
        tell(barrier, peer)
    low = z < 4
    for c in range(2):
        for collector, when in ((COLLECT_LOW + c, low), (COLLECT_ALL + c, True)):

            @pl.when(jnp.logical_and(me != collector, when))
            def _():
                tell(barrier, {"tm": collector})

    for copy in own + tables_in:
        copy.start()
    collects_low, collects_all = me // 2 == COLLECT_LOW // 2, me // 2 == COLLECT_ALL // 2
    heard = jnp.where(collects_low, STEPS // 2 - 1, 0) + jnp.where(collects_all, STEPS - 1, 0)
    pl.semaphore_wait(barrier, len(greeted) + heard)

    @pl.when(collects_low)
    def _():
        for dy in range(8):
            for plane in range(4):
                if 16 * dy + 2 * plane != COLLECT_LOW:
                    tell(ready.at[0], {"tm": 16 * dy + 2 * plane + core})
        pl.semaphore_signal(ready.at[0], inc=1)

    @pl.when(collects_all)
    def _():
        for dy, dz, dc in FAR_FIRST:
            if dc == 0:
                tell(ready.at[1], {"tm": (y + dy) % 8 * 16 + (z + dz) % 8 * 2 + core})
        pl.semaphore_signal(ready.at[1], inc=1)

    def remote(i, a, b, peer):
        return pltpu.make_async_remote_copy(
            a, b, send_sem.at[i], recv_sem.at[i], device_id=peer, device_id_type=MESH
        )

    def rows(ref, first, count):
        return ref.at[pl.ds(first, count)]

    it_own, src_own = it_in.at[0], src_in.at[0]

    def previous(value):
        return [
            remote(0, value, rows(prv, 8, ROWS), {"tm": after}),
            remote(1, rows(value, ROWS - HALO, HALO), rows(prv, TOP, HALO), {"tm": after, "rows": down}),
            remote(2, rows(value, 0, HALO), rows(prv, 8 + ROWS, HALO), {"tm": after, "rows": up}),
        ]

    @pl.when(me < STEPS - 1)
    def _():
        for copy in previous(it_own):
            copy.start()

    @pl.when(me == STEPS - 1)
    def _():
        for copy in previous(ini_in):
            copy.start()

    halos = [
        remote(3, rows(it_own, ROWS - HALO - 1, HALO + 1), rows(it, TOP - 1, HALO + 1), {"rows": down}),
        remote(4, rows(it_own, 0, HALO + 1), rows(it, 8 + ROWS, HALO + 1), {"rows": up}),
        remote(5, rows(src_own, ROWS - HALO, HALO), rows(src, TOP, HALO), {"rows": down}),
        remote(6, rows(src_own, 0, HALO), rows(src, 8 + ROWS, HALO), {"rows": up}),
        remote(7, rows(cnd_in, ROWS - HALO, HALO), cnd.at[pl.ds(TOP, HALO), inside], {"rows": down}),
        remote(8, rows(cnd_in, 0, HALO), cnd.at[pl.ds(8 + ROWS, HALO), inside], {"rows": up}),
    ]
    for copy in halos:
        copy.start()
    for copy in own:
        copy.wait()
    for copy in previous(ini_in) + halos:
        copy.wait()

    @pl.when(slab == 0)
    def _():
        for ref in (it, src, prv, cnd):
            ref[0:8, :] = jnp.zeros((8, ref.shape[1]), jnp.float32)

    @pl.when(slab == 3)
    def _():
        for ref in (it, src, prv, cnd):
            ref[8 + ROWS :, :] = jnp.zeros((8, ref.shape[1]), jnp.float32)

    residual_pack_send(me, y, z, core, it, src, prv, cnd, res, out, inc, a2a_sem, self_sem.at[0], ready)
    packed = own_conductivity(me, y, cnd)

    def wait_all(a, b, depth, sems, sem):
        share = (STEPS - 1) * depth
        pltpu.make_async_copy(rows(a, 0, depth), rows(b, 0, depth), sem).wait()
        pltpu.make_async_remote_copy(
            rows(a, 0, share), rows(b, 0, share), sems.at[0], sems.at[1],
            device_id={"tm": after}, device_id_type=MESH,
        ).wait()

    for copy in tables_in:
        copy.wait()
    prepare(packed, coef, shifts)
    wait_all(out, inc, DEPTH, a2a_sem, self_sem.at[0])
    solve(inc, spec, coef, matrices, select, out2)

    mine = pl.ds(pl.multiple_of(8 * me, 8), 2)
    pltpu.make_async_copy(out2.at[mine], back_ref.at[mine], self_sem.at[1]).start()

    for dy, dz, dc in FAR_FIRST:
        peer = (y + dy) % 8 * 16 + (z + dz) % 8 * 2 + (core + dc) % 2
        pltpu.make_async_remote_copy(
            out2.at[pl.ds(pl.multiple_of(8 * peer, 8), 2)], back_ref.at[mine],
            a2a2_sem.at[0], a2a2_sem.at[1], device_id={"tm": peer}, device_id_type=MESH,
        ).start()

    wait_all(out2, back_ref, 2, a2a2_sem, self_sem.at[1])


def unpack_kernel(back, out, rows):
    block = lax.broadcasted_iota(jnp.int32, (8, 128), 1) // 8
    for h in range(2):
        v = [back[pl.ds(8 * tile + h, 8, stride=128), :] for tile in range(16)]
        for bit in (1, 2, 4, 8):
            there = (block & bit) != 0
            for tile in range(16):
                if not tile & bit:
                    p, q = v[tile], v[tile + bit]
                    v[tile] = jnp.where(there, pltpu.roll(q, 8 * bit, 1), p)
                    v[tile + bit] = jnp.where(there, q, pltpu.roll(p, 128 - 8 * bit, 1))
        for i in range(16):
            row = 16 * h + i
            rows[pl.ds(64 * (row // 8) + row % 8, 8, stride=8), :] = v[i]
    for i in range(ROWS // 8):
        for group in range(8):
            out[0, 8 * i : 8 * i + 8, 128 * group : 128 * group + 128] = rows[
                64 * i + 8 * group : 64 * i + 8 * group + 8
            ]


def shards(source_term, iterate, initial, conductivity):
    shifts, matrices, select = tables()
    f32 = jnp.float32
    dma = pltpu.SemaphoreType.DMA
    back = pl.pallas_call(
        main_kernel,
        out_shape=jax.ShapeDtypeStruct((1024, 128), f32),
        in_specs=[pl.BlockSpec(memory_space=pl.ANY)] * 7,
        out_specs=pl.BlockSpec(memory_space=pl.ANY),
        scratch_shapes=[
            pltpu.VMEM((FRAME, COLS), f32),
            pltpu.VMEM((FRAME, COLS), f32),
            pltpu.VMEM((FRAME, COLS), f32),
            pltpu.VMEM((FRAME, COLS + 256), f32),
            pltpu.VMEM((FRAME, COLS + 256), f32),
            pltpu.VMEM((1024, 128), f32),
            pltpu.VMEM((1024, 128), f32),
            pltpu.VMEM((128, DEPTH * 128), f32),
            pltpu.VMEM((3, 128, DEPTH * 128), f32),
            pltpu.VMEM((1024, 128), f32),
            pltpu.VMEM(shifts.shape, f32),
            pltpu.VMEM(matrices.shape, jnp.bfloat16),
            pltpu.VMEM(select.shape, jnp.bfloat16),
            dma((9,)), dma((9,)), dma((3,)), dma((3,)), dma((2,)), dma((2,)), dma((2,)),
            pltpu.SemaphoreType.REGULAR((2,)),
        ],
        compiler_params=pltpu.CompilerParams(collective_id=0, has_side_effects=True),
        name="main",
    )(source_term, iterate, initial, conductivity, shifts, matrices, select)
    return pl.pallas_call(
        unpack_kernel,
        out_shape=jax.ShapeDtypeStruct((1, ROWS, COLS), f32),
        in_specs=[pl.BlockSpec(memory_space=pltpu.VMEM)],
        out_specs=pl.BlockSpec(memory_space=pltpu.VMEM),
        scratch_shapes=[pltpu.VMEM((8 * ROWS, 128), f32)],
        name="unpack",
    )(back)


def solution(mesh):
    in_specs = (P("tm", "rows", None), P("tm", "rows", None), P("rows", None), P("rows", None))
    out_specs = P("tm", "rows", None)
    return jax.shard_map(shards, mesh=mesh, in_specs=in_specs, out_specs=out_specs, check_vma=False)
```
